256 devices in a mesh: tm: 8 (over z_hi, x), space: 32 (over z_lo, y, core).
Axes of the slice: x: 4, y: 4, z: 8 (z_hi: 2, z_lo: 4; z = z_hi * 4 + z_lo), core: 2. Of those that a mesh axis runs over, the one named last changes fastest.
Arguments:
- queries: bfloat16 [98304, 2240], P(('tm', 'space')), may hold values from -6 to 6
- keys: bfloat16 [98304, 2240], P(('tm', 'space')), may hold values from -6 to 6
- values: bfloat16 [98304, 2240], P(('tm', 'space')), may hold values from -6 to 6
- out_grad: bfloat16 [98304, 2240], P(('tm', 'space')), may hold values from -3584 to 3584
Outputs:
- query_grad: bfloat16 [98304, 2240], P(('tm', 'space'))
- key_grad: bfloat16 [98304, 2240], P(('tm', 'space'))
- value_grad: bfloat16 [98304, 2240], P(('tm', 'space'))
The draws below stay inside these ranges and needn't reach their ends.
All inputs are finite; a program needn't handle non-finite values.
Results may differ from the reference program's by a relative error of at most 0.003.
Values sent between devices are 32-bit elements; how exact they have to be, the bound alone decides.
A program may use at most 64 MiB of HBM per device.

```python
import jax
import jax.numpy as jnp
from jax import lax

HEADS = 20
HEAD = 112
TOK_DEV = 384
WIDTH = 2240
TOKENS = 98304
N_TM = 8
N_SPACE = 32


def level_of(stream_key, dims, pieces, low, top_value):
    def one(position, shards_of):
        heights = jax.random.uniform(jax.random.fold_in(jax.random.fold_in(stream_key, 6), position), (shards_of,), jnp.float32, low / len(pieces), top_value / len(pieces))
        return jnp.repeat(jnp.exp(heights), dims[position] // shards_of).reshape((-1,) + (1,) * (len(dims) - position - 1))

    gain = one(*pieces[0])
    for cut in pieces[1:]:
        gain = gain * one(*cut)
    return gain


def bell_draw(rng, dims, scale, most, cuts=(), held_as=jnp.bfloat16):
    values = jax.random.normal(rng, dims, jnp.float32) * scale
    if len(cuts) > 0:
        values = level_of(rng, dims, cuts, -0.22, 0.18) * values
    return jnp.clip(values, min=-most, max=most).astype(held_as)


def setup_inputs(seed: int = 0) -> dict:
    seeds = jax.random.split(jax.random.key(seed), 5)
    return {
        "queries": bell_draw(seeds[0], (TOKENS, WIDTH), 1.0, 6.0, ((0, 256),)),
        "keys": bell_draw(seeds[1], (TOKENS, WIDTH), 1.0, 6.0, ((0, 256),)),
        "values": bell_draw(seeds[2], (TOKENS, WIDTH), 1.0, 6.0, ((0, 256),)),
        "out_grad": bell_draw(seeds[3], (TOKENS, WIDTH), ((HEAD * TOK_DEV * N_SPACE // 4) ** 0.5), 3584.0, ((0, 256),)),
    }


highest = lax.Precision.HIGHEST


def reference(queries, keys, values, out_grad):
    blocks = N_TM
    per_block = TOK_DEV * N_SPACE
    width = HEADS * HEAD

    def split(array):
        return array.reshape(blocks, per_block, HEADS, HEAD)

    query_blocks = split(queries)
    key_blocks = split(keys)
    value_blocks = split(values)
    grad_blocks = split(out_grad)

    def block_sums(items):
        key_block, value_block = items
        feat_key = jnp.maximum(key_block.astype(jnp.float32), 0.0)
        key_state = jnp.einsum("thi,thj->hij", feat_key, value_block.astype(jnp.float32), precision=highest)
        return key_state, jnp.sum(feat_key, axis=0)

    local_states, local_norms = lax.map(block_sums, (key_blocks, value_blocks))
    states = jnp.cumsum(local_states, axis=0)
    norms = jnp.cumsum(local_norms, axis=0)

    def query_side(items):
        query_block, grad_block, key_state, key_norm = items
        query_float = query_block.astype(jnp.float32)
        feat_query = jnp.maximum(query_float, 0.0)
        grad_heads = grad_block.astype(jnp.float32)
        numer = jnp.einsum("thi,hij->thj", feat_query, key_state, precision=highest)
        denom = jnp.einsum("thi,hi->th", feat_query, key_norm, precision=highest) + 1.0
        output = numer / denom[..., None]
        grad_numer = grad_heads / denom[..., None]
        grad_denom = -jnp.sum(grad_heads * output, axis=-1) / denom
        grad_feat = jnp.einsum("thj,hij->thi", grad_numer, key_state, precision=highest) + grad_denom[..., None] * key_norm[None]
        query_grad = jnp.where(query_float > 0, grad_feat, 0.0).astype(jnp.bfloat16)
        back_state = jnp.einsum("thi,thj->hij", feat_query, grad_numer, precision=highest)
        back_norm = jnp.sum(feat_query * grad_denom[..., None], axis=0)
        return query_grad, back_state, back_norm

    query_grads, back_states, back_norms = lax.map(query_side, (query_blocks, grad_blocks, states, norms))
    suffix_states = jnp.flip(jnp.cumsum(jnp.flip(back_states, 0), axis=0), 0)
    suffix_norms = jnp.flip(jnp.cumsum(jnp.flip(back_norms, 0), axis=0), 0)

    def key_side(items):
        key_block, value_block, grad_state, grad_norm = items
        key_float = key_block.astype(jnp.float32)
        feat_key = jnp.maximum(key_float, 0.0)
        value_float = value_block.astype(jnp.float32)
        value_grad = jnp.einsum("thi,hij->thj", feat_key, grad_state, precision=highest)
        key_feat = jnp.einsum("thj,hij->thi", value_float, grad_state, precision=highest) + grad_norm[None]
        key_grad = jnp.where(key_float > 0, key_feat, 0.0)
        return key_grad.astype(jnp.bfloat16), value_grad.astype(jnp.bfloat16)

    key_grads, value_grads = lax.map(key_side, (key_blocks, value_blocks, suffix_states, suffix_norms))
    total = blocks * per_block
    return (query_grads.reshape(total, width), key_grads.reshape(total, width), value_grads.reshape(total, width))
```

```python
import functools

import jax
import jax.numpy as jnp
from jax import lax
from jax.experimental import pallas as pl
from jax.experimental.pallas import tpu as pltpu
from jax.sharding import PartitionSpec as P

HEADS = 20
HEAD = 112
LANES = 128
N_X, N_ZH, N_Z, N_Y, N_C = 4, 2, 4, 4, 2
MESH = pl.DeviceIdType.MESH
F32, BF16 = jnp.float32, jnp.bfloat16


def place(h):
    tile, offset = divmod(HEAD * h, LANES)
    return tile, offset, max(offset + HEAD - LANES, 0)


def spare_lane(h):
    return (HEAD * (h + 1)) % LANES


def lane_index():
    return lax.broadcasted_iota(jnp.int32, (1, LANES), 1)


def tile_of(ref, tile):
    start, width = LANES * tile, ref.shape[1]
    if start + LANES <= width:
        return ref[:, start : start + LANES]
    part = ref[:, start:width]
    return jnp.concatenate([part, jnp.zeros((part.shape[0], LANES - part.shape[1]), part.dtype)], 1)


def folded(ref, h, spare=0.0):
    tile, offset, over = place(h)
    lane = lane_index()
    rest = jnp.zeros((1, LANES), F32)
    if spare:
        rest = jnp.where(lane == spare_lane(h), spare, rest)
    rest = jnp.broadcast_to(rest.astype(ref.dtype), (ref.shape[0], LANES))
    first = tile_of(ref, tile)
    if offset + HEAD > LANES:
        return jnp.where(lane >= offset, first, jnp.where(lane < over, tile_of(ref, tile + 1), rest))
    return jnp.where((lane >= offset) & (lane < offset + HEAD), first, rest)


def store_rows(ref, h, square):
    _, offset, over = place(h)
    base = HEAD * h
    head = min(LANES - offset, HEAD)
    ref[base : base + head, :] = square[offset : offset + head, :]
    if over:
        ref[base + head : base + HEAD, :] = square[:over, :]


def load_rows(ref, h):
    _, offset, over = place(h)
    base = HEAD * h
    head = min(LANES - offset, HEAD)
    blank = jnp.zeros((LANES - HEAD, LANES), F32)
    parts = []
    if over:
        parts = [ref[base + head : base + HEAD, :], blank, ref[base : base + head, :]]
    elif offset:
        parts = [blank, ref[base : base + head, :]]
    else:
        parts = [ref[base : base + head, :], blank]
    return jnp.concatenate(parts, 0)


def halves(x):
    high = x.astype(BF16)
    low = (x - high.astype(F32)).astype(BF16)
    return high, low


def emit(ref, h, result, before):
    tile, offset, over = place(h)
    width = ref.shape[1]
    if offset:
        ref[:, LANES * tile : LANES * (tile + 1)] = jnp.where(lane_index() < offset, before, result)
    if h == HEADS - 1:
        ref[:, LANES * (tile + 1) : width] = result[:, : width - LANES * (tile + 1)]


def dot(a, b, contract):
    return lax.dot_general(a, b, ((contract[:1], contract[1:]), ((), ())), preferred_element_type=F32)


def key_state(k_ref, v_ref, s_ref):
    for h in range(HEADS):
        feat = jnp.maximum(folded(k_ref, h), 0)
        store_rows(s_ref, h, dot(feat, folded(v_ref, h, 1.0), (0, 0)))
    s_ref[HEADS * HEAD :, :] = jnp.zeros((s_ref.shape[0] - HEADS * HEAD, LANES), F32)


def query_side(q_ref, g_ref, s_ref, dq_ref, r_ref):
    before = None
    for h in range(HEADS):
        spare = spare_lane(h)
        lane = lane_index()
        feat = jnp.maximum(folded(q_ref, h), 0)
        grad = folded(g_ref, h)
        state = load_rows(s_ref, h)
        high, low = halves(state)
        both = jnp.concatenate([high, low], 1)
        spread = jnp.broadcast_to(state[:, spare : spare + 1], (LANES, LANES))
        den = dot(jnp.concatenate([feat, feat], 1), jnp.concatenate(halves(spread), 0), (1, 0)) + 1.0
        inv = 1.0 / den
        back = dot(jnp.concatenate([grad, grad], 1), both, (1, 1))
        pick = jnp.broadcast_to((lane == spare).astype(F32).astype(BF16), (16, LANES))
        norm = dot(jnp.concatenate([pick, pick], 1), both, (1, 1))[:1]
        feat32 = feat.astype(F32)
        along = jnp.sum(feat32 * back, axis=1, keepdims=True)
        grad_den = -(along * inv) * inv
        result = jnp.where(feat32 > 0, back * inv + grad_den * norm, 0.0).astype(BF16)
        emit(dq_ref, h, result, before)
        before = result
        scaled = jnp.where(lane == spare, grad_den, grad.astype(F32) * inv)
        pair = dot(feat, jnp.concatenate(halves(scaled), 1), (0, 0))
        store_rows(r_ref, h, pair[:, :LANES] + pair[:, LANES:])
    r_ref[HEADS * HEAD :, :] = jnp.zeros((r_ref.shape[0] - HEADS * HEAD, LANES), F32)


def key_side(k_ref, v_ref, r_ref, dk_ref, dv_ref):
    before_k = before_v = None
    for h in range(HEADS):
        feat = jnp.maximum(folded(k_ref, h), 0)
        value = folded(v_ref, h, 1.0)
        high, low = halves(load_rows(r_ref, h))
        grad_v = dot(jnp.concatenate([feat, feat], 1), jnp.concatenate([high, low], 0), (1, 0))
        grad_k = dot(jnp.concatenate([value, value], 1), jnp.concatenate([high, low], 1), (1, 1))
        grad_v = grad_v.astype(BF16)
        grad_k = jnp.where(feat.astype(F32) > 0, grad_k, 0.0).astype(BF16)
        emit(dv_ref, h, grad_v, before_v)
        emit(dk_ref, h, grad_k, before_k)
        before_k, before_v = grad_k, grad_v


def exchange(
    reverse, s_ref, g_ref, from_core, on_chip, from_y, to_z, own, from_z, share, from_x, total, from_half,
    core_s, core_r, y_s, y_r, z_s, z_r, x_s, x_r, half_s, half_r, zg_s, zg_r, yg_s, yg_r, cg_s, cg_r,
):
    tm, space = lax.axis_index("tm"), lax.axis_index("space")
    zh, x = lax.div(tm, N_X), lax.rem(tm, N_X)
    z, rest = lax.div(space, N_Y * N_C), lax.rem(space, N_Y * N_C)
    y, c = lax.div(rest, N_C), lax.rem(rest, N_C)

    def at(zh=zh, x=x, z=z, y=y, c=c):
        return (zh * N_X + x, (z * N_Y + y) * N_C + c)

    def turn(v, k, n):
        return lax.rem(v + (k + n), n)

    mate = at(c=1 - c)
    other = at(zh=1 - zh)
    peers_y = [at(y=turn(y, j, N_Y)) for j in range(1, N_Y)]
    peers_z = [at(z=turn(z, j, N_Z)) for j in range(1, N_Z)]
    peers_x = [at(x=turn(x, j, N_X)) for j in range(1, N_X)]

    barrier = pltpu.get_barrier_semaphore()
    everyone = [mate, other, *peers_y, *peers_z, *peers_x]
    for peer in everyone:
        pl.semaphore_signal(barrier, inc=1, device_id=peer, device_id_type=MESH)
    pl.semaphore_wait(barrier, len(everyone))

    started = []

    def send(src, dst, send_sem, recv_sem, peer):
        copy = pltpu.make_async_remote_copy(
            src_ref=src, dst_ref=dst, send_sem=send_sem, recv_sem=recv_sem, device_id=peer, device_id_type=MESH
        )
        copy.start()
        started.append(copy)
        return copy

    order = [*range(1, N_Z), 0]
    column = {k: turn(z, k, N_Z) for k in order}
    core = {k: send(s_ref.at[1 - c, column[k]], from_core.at[k], core_s.at[k], core_r.at[k], mate) for k in order}
    ring = {}
    for k in order:
        core[k].wait_recv()
        on_chip[k] = s_ref[c, column[k]] + from_core[k]
        for j, peer in enumerate(peers_y):
            slot = k * (N_Y - 1) + j
            ring[k, j] = send(
                on_chip.at[k, turn(y, j + 1, N_Y)], from_y.at[slot], y_s.at[slot], y_r.at[slot], peer
            )
    line = []
    for k in order:
        value = on_chip[k, y]
        for j in range(N_Y - 1):
            ring[k, j].wait_recv()
            value = value + from_y[k * (N_Y - 1) + j]
        if k:
            to_z[k - 1] = value
            line.append(send(to_z.at[k - 1], from_z.at[k - 1], z_s.at[k - 1], z_r.at[k - 1], peers_z[k - 1]))
        else:
            own[...] = value
    value = own[...]
    for j, copy in enumerate(line):
        copy.wait_recv()
        value = value + from_z[j]
    share[...] = value
    rows = [send(share, from_x.at[j], x_s.at[j], x_r.at[j], peer) for j, peer in enumerate(peers_x)]
    value = share[...]
    for j, copy in enumerate(rows):
        copy.wait_recv()
        value = value + from_x[j]
    total[...] = value
    cross = send(total, from_half, half_s, half_r, other)
    value = share[...]
    for j in range(N_X - 1):
        wanted = x < j + 1 if reverse else x >= j + 1
        value = value + jnp.where(wanted, from_x[j], 0.0)
    cross.wait_recv()
    value = value + jnp.where(zh == (0 if reverse else 1), from_half[...], 0.0)
    g_ref[c, z, y] = value

    spread = {}
    mine = g_ref.at[c, z, y]
    for j, peer in enumerate(peers_z):
        spread[j + 1] = send(mine, mine, zg_s.at[j], zg_r.at[j], peer)
    source = {k: turn(z, -k, N_Z) for k in range(N_Z)}
    ring = {}
    for k in range(N_Z):
        if k:
            spread[k].wait_recv()
        block = g_ref.at[c, source[k], y]
        for j, peer in enumerate(peers_y):
            slot = k * (N_Y - 1) + j
            ring[k, j] = send(block, block, yg_s.at[slot], yg_r.at[slot], peer)
    core = []
    for k in range(N_Z):
        for j in range(N_Y - 1):
            ring[k, j].wait_recv()
        block = g_ref.at[c, source[k]]
        core.append(send(block, block, cg_s.at[k], cg_r.at[k], mate))
    for copy in core:
        copy.wait_recv()
    for copy in started:
        copy.wait_send()


def padded_rows():
    unit = 8 * N_Z * N_Y * N_C
    return -(-HEADS * HEAD // unit) * unit


def carried(state, reverse):
    block = state.shape[0] // (N_C * N_Z * N_Y)
    dims = (N_C, N_Z, N_Y, block, LANES)
    dma = pltpu.SemaphoreType.DMA
    ny, nz, nx = N_Y - 1, N_Z - 1, N_X - 1
    vmem = pl.BlockSpec(memory_space=pltpu.VMEM)
    out = pl.pallas_call(
        functools.partial(exchange, reverse),
        out_shape=jax.ShapeDtypeStruct(dims, F32),
        in_specs=[vmem],
        out_specs=vmem,
        scratch_shapes=[
            pltpu.VMEM((N_Z, N_Y, block, LANES), F32),
            pltpu.VMEM((N_Z, N_Y, block, LANES), F32),
            pltpu.VMEM((N_Z * ny, block, LANES), F32),
            pltpu.VMEM((nz, block, LANES), F32),
            pltpu.VMEM((block, LANES), F32),
            pltpu.VMEM((nz, block, LANES), F32),
            pltpu.VMEM((block, LANES), F32),
            pltpu.VMEM((nx, block, LANES), F32),
            pltpu.VMEM((block, LANES), F32),
            pltpu.VMEM((block, LANES), F32),
            dma((N_Z,)), dma((N_Z,)),
            dma((N_Z * ny,)), dma((N_Z * ny,)),
            dma((nz,)), dma((nz,)),
            dma((nx,)), dma((nx,)),
            dma, dma,
            dma((nz,)), dma((nz,)),
            dma((N_Z * ny,)), dma((N_Z * ny,)),
            dma((N_Z,)), dma((N_Z,)),
        ],
        compiler_params=pltpu.CompilerParams(collective_id=1 if reverse else 0, has_side_effects=True),
        name="suffix_exchange" if reverse else "prefix_exchange",
    )(state.reshape(dims))
    return out.reshape(state.shape)


def local(kernel, outs, name):
    return pl.pallas_call(
        kernel,
        out_shape=outs,
        name=name,
        compiler_params=pltpu.CompilerParams(vmem_limit_bytes=56 * 1024 * 1024),
    )


def on_device(queries, keys, values, out_grad):
    like = jax.ShapeDtypeStruct(queries.shape, BF16)
    state = jax.ShapeDtypeStruct((padded_rows(), LANES), F32)
    s_local = local(key_state, state, "key_state")(keys, values)
    s_full = carried(s_local, False)
    query_grad, r_local = local(query_side, (like, state), "query_side")(queries, out_grad, s_full)
    r_full = carried(r_local, True)
    key_grad, value_grad = local(key_side, (like, like), "key_side")(keys, values, r_full)
    return query_grad, key_grad, value_grad


def solution(mesh):
    spec = P(("tm", "space"), None)
    return jax.shard_map(
        on_device, mesh=mesh, in_specs=(spec,) * 4, out_specs=(spec,) * 3, check_vma=False
    )
```

```python
import functools

import jax
import jax.numpy as jnp
from jax import lax
from jax.experimental import pallas as pl
from jax.experimental.pallas import tpu as pltpu
from jax.sharding import PartitionSpec as P

HEADS = 20
HEAD = 112
LANES = 128
N_X, N_ZH, N_Z, N_Y, N_C = 4, 2, 4, 4, 2
MESH = pl.DeviceIdType.MESH
F32, BF16 = jnp.float32, jnp.bfloat16


def halves(x):
    high = x.astype(BF16)
    low = (x - high.astype(F32)).astype(BF16)
    return high, low


def dot(a, b, contract):
    return lax.dot_general(a, b, ((contract[:1], contract[1:]), ((), ())), preferred_element_type=F32)


def head_rows(h):
    return slice(HEAD * h, HEAD * (h + 1))


def under(rows, first):
    rest = jnp.zeros((LANES - HEAD, rows.shape[1]), F32)
    at = lax.broadcasted_iota(jnp.int32, rest.shape, 0)
    return jnp.concatenate([rows, jnp.where(at == 0, first, rest).astype(rows.dtype)], 0)


def key_state(k_ref, v_ref, s_ref):
    for h in range(HEADS):
        rows = head_rows(h)
        feat = jnp.maximum(k_ref[rows, :], 0)
        s_ref[rows, :] = dot(feat, under(v_ref[rows, :], 1.0), (1, 1))
    s_ref[HEADS * HEAD :, :] = jnp.zeros((s_ref.shape[0] - HEADS * HEAD, LANES), F32)


def query_side(q_ref, g_ref, s_ref, dq_ref, r_ref):
    for h in range(HEADS):
        rows = head_rows(h)
        feat = jnp.maximum(q_ref[rows, :], 0)
        feat32 = feat.astype(F32)
        grad = g_ref[rows, :]
        state = s_ref[rows, :]
        norm = state[:, HEAD : HEAD + 1]
        den = jnp.sum(feat32 * norm, axis=0, keepdims=True) + 1.0
        inv = 1.0 / den
        wide = under(grad, 0.0)
        back = dot(jnp.concatenate(halves(state), 1), jnp.concatenate([wide, wide], 0), (1, 0))
        along = jnp.sum(feat32 * back, axis=0, keepdims=True)
        grad_den = -(along * inv) * inv
        dq_ref[rows, :] = jnp.where(feat32 > 0, back * inv + norm * grad_den, 0.0).astype(BF16)
        scaled = under(grad.astype(F32) * inv, grad_den)
        pair = dot(feat, jnp.concatenate(halves(scaled), 0), (1, 1))
        r_ref[rows, :] = pair[:, :LANES] + pair[:, LANES:]
    r_ref[HEADS * HEAD :, :] = jnp.zeros((r_ref.shape[0] - HEADS * HEAD, LANES), F32)


def key_side(k_ref, v_ref, r_ref, dk_ref, dv_ref):
    for h in range(HEADS):
        rows = head_rows(h)
        feat = jnp.maximum(k_ref[rows, :], 0)
        value = under(v_ref[rows, :], 1.0)
        high, low = halves(r_ref[rows, :])
        grad_v = dot(jnp.concatenate([high, low], 0), jnp.concatenate([feat, feat], 0), (0, 0))
        grad_k = dot(jnp.concatenate([high, low], 1), jnp.concatenate([value, value], 0), (1, 0))
        dv_ref[rows, :] = grad_v[:HEAD].astype(BF16)
        dk_ref[rows, :] = jnp.where(feat.astype(F32) > 0, grad_k, 0.0).astype(BF16)


def exchange(
    reverse, s_ref, g_ref, from_core, on_chip, from_y, to_z, own, from_z, share, from_x, total, from_half,
    core_s, core_r, y_s, y_r, z_s, z_r, x_s, x_r, half_s, half_r, zg_s, zg_r, yg_s, yg_r, cg_s, cg_r,
):
    tm, space = lax.axis_index("tm"), lax.axis_index("space")
    zh, x = lax.div(tm, N_X), lax.rem(tm, N_X)
    z, rest = lax.div(space, N_Y * N_C), lax.rem(space, N_Y * N_C)
    y, c = lax.div(rest, N_C), lax.rem(rest, N_C)

    def at(zh=zh, x=x, z=z, y=y, c=c):
        return (zh * N_X + x, (z * N_Y + y) * N_C + c)

    def turn(v, k, n):
        return lax.rem(v + (k + n), n)

    mate = at(c=1 - c)
    other = at(zh=1 - zh)
    peers_y = [at(y=turn(y, j, N_Y)) for j in range(1, N_Y)]
    peers_z = [at(z=turn(z, j, N_Z)) for j in range(1, N_Z)]
    peers_x = [at(x=turn(x, j, N_X)) for j in range(1, N_X)]

    barrier = pltpu.get_barrier_semaphore()
    everyone = [mate, other, *peers_y, *peers_z, *peers_x]
    for peer in everyone:
        pl.semaphore_signal(barrier, inc=1, device_id=peer, device_id_type=MESH)
    pl.semaphore_wait(barrier, len(everyone))

    started = []

    def send(src, dst, send_sem, recv_sem, peer):
        copy = pltpu.make_async_remote_copy(
            src_ref=src, dst_ref=dst, send_sem=send_sem, recv_sem=recv_sem, device_id=peer, device_id_type=MESH
        )
        copy.start()
        started.append(copy)
        return copy

    order = [*range(1, N_Z), 0]
    column = {k: turn(z, k, N_Z) for k in order}
    core = {k: send(s_ref.at[1 - c, column[k]], from_core.at[k], core_s.at[k], core_r.at[k], mate) for k in order}
    ring = {}
    for k in order:
        core[k].wait_recv()
        on_chip[k] = s_ref[c, column[k]] + from_core[k]
        for j, peer in enumerate(peers_y):
            slot = k * (N_Y - 1) + j
            ring[k, j] = send(
                on_chip.at[k, turn(y, j + 1, N_Y)], from_y.at[slot], y_s.at[slot], y_r.at[slot], peer
            )
    line = []
    for k in order:
        value = on_chip[k, y]
        for j in range(N_Y - 1):
            ring[k, j].wait_recv()
            value = value + from_y[k * (N_Y - 1) + j]
        if k:
            to_z[k - 1] = value
            line.append(send(to_z.at[k - 1], from_z.at[k - 1], z_s.at[k - 1], z_r.at[k - 1], peers_z[k - 1]))
        else:
            own[...] = value
    value = own[...]
    for j, copy in enumerate(line):
        copy.wait_recv()
        value = value + from_z[j]
    share[...] = value
    rows = [send(share, from_x.at[j], x_s.at[j], x_r.at[j], peer) for j, peer in enumerate(peers_x)]
    value = share[...]
    for j, copy in enumerate(rows):
        copy.wait_recv()
        value = value + from_x[j]
    total[...] = value
    cross = send(total, from_half, half_s, half_r, other)
    value = share[...]
    for j in range(N_X - 1):
        wanted = x < j + 1 if reverse else x >= j + 1
        value = value + jnp.where(wanted, from_x[j], 0.0)
    cross.wait_recv()
    value = value + jnp.where(zh == (0 if reverse else 1), from_half[...], 0.0)
    g_ref[c, z, y] = value

    spread = {}
    mine = g_ref.at[c, z, y]
    for j, peer in enumerate(peers_z):
        spread[j + 1] = send(mine, mine, zg_s.at[j], zg_r.at[j], peer)
    source = {k: turn(z, -k, N_Z) for k in range(N_Z)}
    ring = {}
    for k in range(N_Z):
        if k:
            spread[k].wait_recv()
        block = g_ref.at[c, source[k], y]
        for j, peer in enumerate(peers_y):
            slot = k * (N_Y - 1) + j
            ring[k, j] = send(block, block, yg_s.at[slot], yg_r.at[slot], peer)
    core = []
    for k in range(N_Z):
        for j in range(N_Y - 1):
            ring[k, j].wait_recv()
        block = g_ref.at[c, source[k]]
        core.append(send(block, block, cg_s.at[k], cg_r.at[k], mate))
    for copy in core:
        copy.wait_recv()
    for copy in started:
        copy.wait_send()


def padded_rows():
    unit = 8 * N_Z * N_Y * N_C
    return -(-HEADS * HEAD // unit) * unit


def carried(state, reverse):
    block = state.shape[0] // (N_C * N_Z * N_Y)
    dims = (N_C, N_Z, N_Y, block, LANES)
    dma = pltpu.SemaphoreType.DMA
    ny, nz, nx = N_Y - 1, N_Z - 1, N_X - 1
    vmem = pl.BlockSpec(memory_space=pltpu.VMEM)
    out = pl.pallas_call(
        functools.partial(exchange, reverse),
        out_shape=jax.ShapeDtypeStruct(dims, F32),
        in_specs=[vmem],
        out_specs=vmem,
        scratch_shapes=[
            pltpu.VMEM((N_Z, N_Y, block, LANES), F32),
            pltpu.VMEM((N_Z, N_Y, block, LANES), F32),
            pltpu.VMEM((N_Z * ny, block, LANES), F32),
            pltpu.VMEM((nz, block, LANES), F32),
            pltpu.VMEM((block, LANES), F32),
            pltpu.VMEM((nz, block, LANES), F32),
            pltpu.VMEM((block, LANES), F32),
            pltpu.VMEM((nx, block, LANES), F32),
            pltpu.VMEM((block, LANES), F32),
            pltpu.VMEM((block, LANES), F32),
            dma((N_Z,)), dma((N_Z,)),
            dma((N_Z * ny,)), dma((N_Z * ny,)),
            dma((nz,)), dma((nz,)),
            dma((nx,)), dma((nx,)),
            dma, dma,
            dma((nz,)), dma((nz,)),
            dma((N_Z * ny,)), dma((N_Z * ny,)),
            dma((N_Z,)), dma((N_Z,)),
        ],
        compiler_params=pltpu.CompilerParams(collective_id=1 if reverse else 0, has_side_effects=True),
        name="suffix_exchange" if reverse else "prefix_exchange",
    )(state.reshape(dims))
    return out.reshape(state.shape)


def local(kernel, outs, name):
    return pl.pallas_call(
        kernel,
        out_shape=outs,
        name=name,
        compiler_params=pltpu.CompilerParams(vmem_limit_bytes=56 * 1024 * 1024),
    )


def on_device(queries, keys, values, out_grad):
    queries, keys, values, out_grad = queries.T, keys.T, values.T, out_grad.T
    like = jax.ShapeDtypeStruct(queries.shape, BF16)
    state = jax.ShapeDtypeStruct((padded_rows(), LANES), F32)
    s_local = local(key_state, state, "key_state")(keys, values)
    s_full = carried(s_local, False)
    query_grad, r_local = local(query_side, (like, state), "query_side")(queries, out_grad, s_full)
    r_full = carried(r_local, True)
    key_grad, value_grad = local(key_side, (like, like), "key_side")(keys, values, r_full)
    return query_grad.T, key_grad.T, value_grad.T


def solution(mesh):
    spec = P(("tm", "space"), None)
    return jax.shard_map(
        on_device, mesh=mesh, in_specs=(spec,) * 4, out_specs=(spec,) * 3, check_vma=False
    )
```

```python
import functools

import jax
import jax.numpy as jnp
from jax import lax
from jax.experimental import pallas as pl
from jax.experimental.pallas import tpu as pltpu
from jax.sharding import PartitionSpec as P

HEADS = 20
HEAD = 112
LANES = 128
N_X, N_ZH, N_Z, N_Y, N_C = 4, 2, 4, 4, 2
BLOCK = 8 * -(-HEADS * HEAD // (8 * N_Z * N_Y * N_C))
ROWS = BLOCK * N_Z * N_Y * N_C
SMALL = 8 * -(-HEADS // 8)
GROUP = 4
MESH = pl.DeviceIdType.MESH
F32, BF16 = jnp.float32, jnp.bfloat16
ORDER = [*range(1, N_Z), 0]


def halves(x):
    high = x.astype(BF16)
    low = (x - high.astype(F32)).astype(BF16)
    return high, low


def dot(a, b, contract):
    return lax.dot_general(a, b, ((contract[:1], contract[1:]), ((), ())), preferred_element_type=F32)


def head_rows(h):
    return slice(HEAD * h, HEAD * (h + 1))


def under(rows, first):
    rest = jnp.zeros((LANES - HEAD, rows.shape[1]), F32)
    at = lax.broadcasted_iota(jnp.int32, rest.shape, 0)
    return jnp.concatenate([rows, jnp.where(at == 0, first, rest).astype(rows.dtype)], 0)


def split_rows(row):
    high, low = halves(row)
    at = lax.broadcasted_iota(jnp.int32, (16, row.shape[1]), 0)
    return jnp.where(at < 8, high.astype(F32), low.astype(F32)).astype(BF16)


def fold_rows(pair):
    return pair[:1] + pair[8:9]


def turn(v, k, n):
    return lax.rem(v + (k + n), n)


class Wires:
    def __init__(self):
        tm, space = lax.axis_index("tm"), lax.axis_index("space")
        self.zh, self.x = lax.div(tm, N_X), lax.rem(tm, N_X)
        self.z, rest = lax.div(space, N_Y * N_C), lax.rem(space, N_Y * N_C)
        self.y, self.c = lax.div(rest, N_C), lax.rem(rest, N_C)
        self.started = []
        self.mate = self.at(c=1 - self.c)
        self.other = self.at(zh=1 - self.zh)
        self.peers_y = [self.at(y=turn(self.y, j, N_Y)) for j in range(1, N_Y)]
        self.peers_z = [self.at(z=turn(self.z, j, N_Z)) for j in range(1, N_Z)]
        self.peers_x = [self.at(x=turn(self.x, j, N_X)) for j in range(1, N_X)]
        self.near = [
            self.at(y=turn(self.y, j, N_Y), c=turn(self.c, i, N_C))
            for j in range(N_Y) for i in range(N_C) if i or j
        ]
        depth = self.zh * N_Z + self.z
        self.ring = []
        for k in range(1, N_ZH * N_Z):
            d = turn(depth, k, N_ZH * N_Z)
            self.ring.append(self.at(zh=lax.div(d, N_Z), z=lax.rem(d, N_Z)))
        self.same_half = [
            lax.div(turn(depth, -k, N_ZH * N_Z), N_Z) == self.zh for k in range(1, N_ZH * N_Z)
        ]

    def at(self, **moved):
        zh, x, z, y, c = (moved.get(n, getattr(self, n, None)) for n in ("zh", "x", "z", "y", "c"))
        return (zh * N_X + x, (z * N_Y + y) * N_C + c)

    def send(self, src, dst, send_sem, recv_sem, peer):
        copy = pltpu.make_async_remote_copy(
            src_ref=src, dst_ref=dst, send_sem=send_sem, recv_sem=recv_sem, device_id=peer, device_id_type=MESH
        )
        copy.start()
        self.started.append(copy)
        return copy


def block(ref, c, z, y=None):
    start = (c * N_Z + z) * N_Y
    if y is None:
        return ref.at[pl.ds(pl.multiple_of(start * BLOCK, 8), N_Y * BLOCK)]
    return ref.at[pl.ds(pl.multiple_of((start + y) * BLOCK, 8), BLOCK)]


class Flow:
    SCRATCH = [
        pltpu.VMEM((N_Z, N_Y * BLOCK, LANES), F32),
        pltpu.VMEM((N_Z, N_Y * BLOCK, LANES), F32),
        pltpu.VMEM((N_Z * (N_Y - 1), BLOCK, LANES), F32),
        pltpu.VMEM((N_Z, BLOCK, LANES), F32),
        pltpu.VMEM((N_Z - 1, BLOCK, LANES), F32),
        pltpu.VMEM((BLOCK, LANES), F32),
        pltpu.VMEM((N_X - 1, BLOCK, LANES), F32),
        pltpu.VMEM((BLOCK, LANES), F32),
        pltpu.VMEM((BLOCK, LANES), F32),
        pltpu.SemaphoreType.DMA((42,)),
        pltpu.SemaphoreType.DMA((42,)),
    ]

    def __init__(self, wires, reverse, local, full, scratch):
        self.w, self.reverse, self.local, self.full = wires, reverse, local, full
        (self.from_core, self.on_chip, self.from_y, self.to_z, self.from_z, self.share, self.from_x,
         self.total, self.from_half, self.sent, self.got) = scratch
        self.column = {k: turn(wires.z, k, N_Z) for k in ORDER}
        self.source = {k: turn(wires.z, -k, N_Z) for k in range(N_Z)}

    def send(self, src, dst, n, peer):
        return self.w.send(src, dst, self.sent.at[n], self.got.at[n], peer)

    def start(self):
        w = self.w
        self.core = {
            k: self.send(block(self.local, 1 - w.c, self.column[k]), self.from_core.at[k], k, w.mate) for k in ORDER
        }

    def over_y(self):
        w = self.w
        self.over = {}
        for k in ORDER:
            self.core[k].wait_recv()
            self.on_chip[k] = block(self.local, w.c, self.column[k])[...] + self.from_core[k]
            for j, peer in enumerate(w.peers_y):
                slot = k * (N_Y - 1) + j
                piece = pl.ds(pl.multiple_of(turn(w.y, j + 1, N_Y) * BLOCK, 8), BLOCK)
                self.over[k, j] = self.send(self.on_chip.at[k, piece], self.from_y.at[slot], 4 + slot, peer)

    def over_z(self):
        w = self.w
        self.line = []
        mine = pl.ds(pl.multiple_of(w.y * BLOCK, 8), BLOCK)
        for k in ORDER:
            value = self.on_chip[k, mine]
            for j in range(N_Y - 1):
                self.over[k, j].wait_recv()
                value = value + self.from_y[k * (N_Y - 1) + j]
            self.to_z[k] = value
            if k:
                self.line.append(self.send(self.to_z.at[k], self.from_z.at[k - 1], 15 + k, w.peers_z[k - 1]))

    def over_x(self):
        value = self.to_z[0]
        for j, copy in enumerate(self.line):
            copy.wait_recv()
            value = value + self.from_z[j]
        self.share[...] = value
        self.rows = [self.send(self.share, self.from_x.at[j], 19 + j, p) for j, p in enumerate(self.w.peers_x)]

    def over_half(self):
        value = self.share[...]
        for j, copy in enumerate(self.rows):
            copy.wait_recv()
            value = value + self.from_x[j]
        self.total[...] = value
        self.cross = self.send(self.total, self.from_half, 22, self.w.other)

    def gather_z(self):
        w = self.w
        value = self.share[...]
        for j in range(N_X - 1):
            wanted = w.x < j + 1 if self.reverse else w.x >= j + 1
            value = value + jnp.where(wanted, self.from_x[j], 0.0)
        self.cross.wait_recv()
        value = value + jnp.where(w.zh == (0 if self.reverse else 1), self.from_half[...], 0.0)
        mine = block(self.full, w.c, w.z, w.y)
        mine[...] = value
        self.spread = {j + 1: self.send(mine, mine, 23 + j, p) for j, p in enumerate(w.peers_z)}

    def gather_y(self):
        w = self.w
        self.over = {}
        for k in range(N_Z):
            if k:
                self.spread[k].wait_recv()
            piece = block(self.full, w.c, self.source[k], w.y)
            for j, peer in enumerate(w.peers_y):
                slot = k * (N_Y - 1) + j
                self.over[k, j] = self.send(piece, piece, 26 + slot, peer)

    def gather_core(self):
        w = self.w
        self.last = []
        for k in range(N_Z):
            for j in range(N_Y - 1):
                self.over[k, j].wait_recv()
            piece = block(self.full, w.c, self.source[k])
            self.last.append(self.send(piece, piece, 38 + k, w.mate))

    def finish(self):
        for copy in self.last:
            copy.wait_recv()


class Small:
    SCRATCH = [
        pltpu.VMEM((SMALL, LANES), F32),
        pltpu.VMEM((N_Y * N_C - 1, SMALL, LANES), F32),
        pltpu.VMEM((SMALL, LANES), F32),
        pltpu.VMEM((N_ZH * N_Z - 1, SMALL, LANES), F32),
        pltpu.VMEM((2, SMALL, LANES), F32),
        pltpu.VMEM((N_X - 1, 2, SMALL, LANES), F32),
        pltpu.SemaphoreType.DMA((17,)),
        pltpu.SemaphoreType.DMA((17,)),
    ]

    def __init__(self, wires, reverse, full, scratch):
        self.w, self.reverse, self.full = wires, reverse, full
        self.local, self.from_near, self.near, self.from_ring, self.both, self.from_x, self.sent, self.got = scratch

    def send(self, src, dst, n, peer):
        return self.w.send(src, dst, self.sent.at[n], self.got.at[n], peer)

    def start(self):
        self.copies = [
            self.send(self.local, self.from_near.at[j], j, peer) for j, peer in enumerate(self.w.near)
        ]

    def over_z(self):
        value = self.local[...]
        for j, copy in enumerate(self.copies):
            copy.wait_recv()
            value = value + self.from_near[j]
        self.near[...] = value
        self.copies = [
            self.send(self.near, self.from_ring.at[j], 7 + j, peer) for j, peer in enumerate(self.w.ring)
        ]

    def over_x(self):
        here, there = self.near[...], jnp.zeros((SMALL, LANES), F32)
        for j, copy in enumerate(self.copies):
            copy.wait_recv()
            piece, same = self.from_ring[j], self.w.same_half[j]
            here = here + jnp.where(same, piece, 0.0)
            there = there + jnp.where(same, 0.0, piece)
        self.both[0] = here
        self.both[1] = there
        self.copies = [
            self.send(self.both, self.from_x.at[j], 14 + j, peer) for j, peer in enumerate(self.w.peers_x)
        ]

    def finish(self):
        w = self.w
        value, far = self.both[0], self.both[1]
        for j, copy in enumerate(self.copies):
            copy.wait_recv()
            wanted = w.x < j + 1 if self.reverse else w.x >= j + 1
            value = value + jnp.where(wanted, self.from_x[j, 0], 0.0)
            far = far + self.from_x[j, 1]
        self.full[...] = value + jnp.where(w.zh == (0 if self.reverse else 1), far, 0.0)


N_FLOW, N_SMALL = len(Flow.SCRATCH), len(Small.SCRATCH)


def whole(k_hbm, v_hbm, q_hbm, g_hbm, dq_hbm, r_full, y_full, *scratch):
    k_ref, v_ref, q_ref, g_ref, dq_ref, s_local, r_local, s_full, z_full, inv_ref, io = scratch[:11]
    scratch = scratch[11:]
    loads = [
        pltpu.make_async_copy(src, dst, io.at[n])
        for n, (src, dst) in enumerate([(k_hbm, k_ref), (v_hbm, v_ref), (q_hbm, q_ref), (g_hbm, g_ref)])
    ]
    for load in loads:
        load.start()
    wires = Wires()
    s = Flow(wires, False, s_local, s_full, scratch[:N_FLOW])
    r = Flow(wires, True, r_local, r_full, scratch[N_FLOW : 2 * N_FLOW])
    z = Small(wires, False, z_full, scratch[2 * N_FLOW : 2 * N_FLOW + N_SMALL])
    y = Small(wires, True, y_full, scratch[2 * N_FLOW + N_SMALL :])

    barrier = pltpu.get_barrier_semaphore()
    everyone = [*wires.near, *wires.ring, *wires.peers_x]
    for peer in everyone:
        pl.semaphore_signal(barrier, inc=1, device_id=peer, device_id_type=MESH)

    tokens = k_ref.shape[1]
    ones = jnp.ones((16, tokens), BF16)
    loads[0].wait()
    z.local[...] = jnp.zeros((SMALL, LANES), F32)
    for h in range(HEADS):
        z.local[h : h + 1, :HEAD] = dot(ones, jnp.maximum(k_ref[head_rows(h), :], 0), (1, 1))[:1]
    pl.semaphore_wait(barrier, len(everyone))
    z.start()

    loads[1].wait()
    for h in range(HEADS):
        rows = head_rows(h)
        s_local[rows, :] = dot(jnp.maximum(k_ref[rows, :], 0), under(v_ref[rows, :], 1.0), (1, 1))
    for local in (s_local, r_local):
        local[HEADS * HEAD :, :] = jnp.zeros((ROWS - HEADS * HEAD, LANES), F32)
    s.start()
    z.over_z()
    s.over_y()
    z.over_x()
    loads[2].wait()
    loads[3].wait()
    z.finish()

    for h in range(HEADS):
        rows = head_rows(h)
        feat = jnp.maximum(q_ref[rows, :], 0)
        den = fold_rows(dot(split_rows(z_full[h : h + 1, :HEAD]), feat, (1, 0))) + 1.0
        inv = 1.0 / den
        inv_ref[h : h + 1, :] = inv
        scaled = under(g_ref[rows, :].astype(F32) * inv, 0.0)
        pair = dot(feat, jnp.concatenate(halves(scaled), 0), (1, 1))
        r_local[rows, :] = pair[:, :LANES] + pair[:, LANES:]
    r.start()
    s.over_z()
    s.over_x()
    r.over_y()
    s.over_half()
    s.gather_z()
    r.over_z()
    s.gather_y()
    r.over_x()
    r.over_half()
    s.gather_core()
    s.finish()

    y.local[...] = jnp.zeros((SMALL, LANES), F32)
    for h in range(HEADS):
        rows = head_rows(h)
        feat = jnp.maximum(q_ref[rows, :], 0)
        feat32 = feat.astype(F32)
        inv = inv_ref[h : h + 1, :]
        state = s_full[rows, :]
        wide = under(g_ref[rows, :], 0.0)
        back = dot(jnp.concatenate(halves(state), 1), jnp.concatenate([wide, wide], 0), (1, 0))
        along = jnp.sum(feat32 * back, axis=0, keepdims=True)
        grad_den = -(along * inv) * inv
        norm = state[:, HEAD : HEAD + 1]
        dq_ref[rows, :] = jnp.where(feat32 > 0, back * inv + norm * grad_den, 0.0).astype(BF16)
        y.local[h : h + 1, :HEAD] = fold_rows(dot(split_rows(grad_den), feat, (1, 1)))
    y.start()
    out = pltpu.make_async_copy(dq_ref, dq_hbm, io.at[4])
    out.start()
    r.gather_z()
    y.over_z()
    r.gather_y()
    y.over_x()
    r.gather_core()
    y.finish()
    r.finish()
    out.wait()
    for copy in wires.started:
        copy.wait_send()


def key_side(k_ref, v_ref, r_ref, y_ref, dk_ref, dv_ref):
    first = pl.program_id(0) * GROUP
    ones = jnp.ones((16, k_ref.shape[1]), BF16)
    at = lax.broadcasted_iota(jnp.int32, (16, LANES), 0)
    for n in range(GROUP):
        rows = head_rows(n)
        feat = jnp.maximum(k_ref[rows, :], 0)
        value = under(v_ref[rows, :], 0.0)
        high, low = halves(r_ref[rows, :])
        grad_v = dot(jnp.concatenate([high, low], 0), jnp.concatenate([feat, feat], 0), (0, 0))
        grad_k = dot(jnp.concatenate([high, low], 1), jnp.concatenate([value, value], 0), (1, 0))
        up, down = (part.astype(F32) for part in halves(y_ref[pl.ds(first + n, 1), :]))
        bias = jnp.where(at == 0, up, jnp.where(at == 1, down, 0.0)).astype(BF16)
        grad_k = grad_k + dot(bias, ones, (0, 0))[:HEAD]
        dv_ref[rows, :] = grad_v[:HEAD].astype(BF16)
        dk_ref[rows, :] = jnp.where(feat.astype(F32) > 0, grad_k, 0.0).astype(BF16)


def on_device(queries, keys, values, out_grad):
    queries, keys, values, out_grad = queries.T, keys.T, values.T, out_grad.T
    width, tokens = queries.shape
    like = jax.ShapeDtypeStruct((width, tokens), BF16)
    anywhere = pl.BlockSpec(memory_space=pl.ANY)
    vmem = pl.BlockSpec(memory_space=pltpu.VMEM)
    query_grad, r_full, y_full = pl.pallas_call(
        whole,
        out_shape=(like, jax.ShapeDtypeStruct((ROWS, LANES), F32), jax.ShapeDtypeStruct((SMALL, LANES), F32)),
        in_specs=[anywhere] * 4,
        out_specs=(anywhere, vmem, vmem),
        scratch_shapes=[
            *[pltpu.VMEM((width, tokens), BF16)] * 5,
            *[pltpu.VMEM((ROWS, LANES), F32)] * 3,
            pltpu.VMEM((SMALL, LANES), F32),
            pltpu.VMEM((SMALL, tokens), F32),
            pltpu.SemaphoreType.DMA((5,)),
            *Flow.SCRATCH, *Flow.SCRATCH, *Small.SCRATCH, *Small.SCRATCH,
        ],
        compiler_params=pltpu.CompilerParams(
            collective_id=0, has_side_effects=True, vmem_limit_bytes=60 * 1024 * 1024
        ),
        name="whole",
    )(keys, values, queries, out_grad)
    rows = pl.BlockSpec((GROUP * HEAD, tokens), lambda i: (i, 0))
    key_grad, value_grad = pl.pallas_call(
        key_side,
        grid=(HEADS // GROUP,),
        out_shape=(like, like),
        in_specs=[
            rows, rows,
            pl.BlockSpec((GROUP * HEAD, LANES), lambda i: (i, 0)),
            pl.BlockSpec((SMALL, LANES), lambda i: (0, 0)),
        ],
        out_specs=(rows, rows),
        name="key_side",
        compiler_params=pltpu.CompilerParams(vmem_limit_bytes=60 * 1024 * 1024),
    )(keys, values, r_full, y_full)
    return query_grad.T, key_grad.T, value_grad.T


def solution(mesh):
    spec = P(("tm", "space"), None)
    return jax.shard_map(
        on_device, mesh=mesh, in_specs=(spec,) * 4, out_specs=(spec,) * 3, check_vma=False
    )
```

```python
import functools

import jax
import jax.numpy as jnp
from jax import lax
from jax.experimental import pallas as pl
from jax.experimental.pallas import tpu as pltpu
from jax.sharding import PartitionSpec as P

HEADS = 20
HEAD = 112
LANES = 128
N_X, N_ZH, N_Z, N_Y, N_C = 4, 2, 4, 4, 2
BLOCK = 8 * -(-HEADS * HEAD // (8 * N_Z * N_Y * N_C))
ROWS = BLOCK * N_Z * N_Y * N_C
SMALL = 8 * -(-HEADS // 8)
GROUP = 4
WHOLE_VMEM = 26 * 1024 * 1024
LAST_VMEM = 24 * 1024 * 1024
MESH = pl.DeviceIdType.MESH
F32, BF16 = jnp.float32, jnp.bfloat16
ORDER = [*range(1, N_Z), 0]


def halves(x):
    high = x.astype(BF16)
    low = (x - high.astype(F32)).astype(BF16)
    return high, low


def dot(a, b, contract):
    return lax.dot_general(a, b, ((contract[:1], contract[1:]), ((), ())), preferred_element_type=F32)


def head_rows(h):
    return slice(HEAD * h, HEAD * (h + 1))


def under(rows, first):
    rest = jnp.zeros((LANES - HEAD, rows.shape[1]), F32)
    at = lax.broadcasted_iota(jnp.int32, rest.shape, 0)
    return jnp.concatenate([rows, jnp.where(at == 0, first, rest).astype(rows.dtype)], 0)


def lane_sums(x):
    parts = [x[:, at : at + LANES] for at in range(0, x.shape[1], LANES)]
    return jnp.sum(sum(parts[1:], parts[0]), axis=1, keepdims=True)


def as_rows(columns):
    blank = jnp.zeros((LANES - HEAD, LANES), F32)
    return jnp.concatenate([columns, blank], 0).T[:SMALL]


def turn(v, k, n):
    return lax.rem(v + (k + n), n)


class Wires:
    def __init__(self):
        tm, space = lax.axis_index("tm"), lax.axis_index("space")
        self.zh, self.x = lax.div(tm, N_X), lax.rem(tm, N_X)
        self.z, rest = lax.div(space, N_Y * N_C), lax.rem(space, N_Y * N_C)
        self.y, self.c = lax.div(rest, N_C), lax.rem(rest, N_C)
        self.started = []
        self.mate = self.at(c=1 - self.c)
        self.other = self.at(zh=1 - self.zh)
        self.peers_y = [self.at(y=turn(self.y, j, N_Y)) for j in range(1, N_Y)]
        self.peers_z = [self.at(z=turn(self.z, j, N_Z)) for j in range(1, N_Z)]
        self.peers_x = [self.at(x=turn(self.x, j, N_X)) for j in range(1, N_X)]
        self.near = [
            self.at(y=turn(self.y, j, N_Y), c=turn(self.c, i, N_C))
            for j in range(N_Y) for i in range(N_C) if i or j
        ]
        depth = self.zh * N_Z + self.z
        self.ring = []
        for k in range(1, N_ZH * N_Z):
            d = turn(depth, k, N_ZH * N_Z)
            self.ring.append(self.at(zh=lax.div(d, N_Z), z=lax.rem(d, N_Z)))
        self.same_half = [
            lax.div(turn(depth, -k, N_ZH * N_Z), N_Z) == self.zh for k in range(1, N_ZH * N_Z)
        ]

    def at(self, **moved):
        zh, x, z, y, c = (moved.get(n, getattr(self, n, None)) for n in ("zh", "x", "z", "y", "c"))
        return (zh * N_X + x, (z * N_Y + y) * N_C + c)

    def send(self, src, dst, send_sem, recv_sem, peer):
        copy = pltpu.make_async_remote_copy(
            src_ref=src, dst_ref=dst, send_sem=send_sem, recv_sem=recv_sem, device_id=peer, device_id_type=MESH
        )
        copy.start()
        self.started.append(copy)
        return copy


def block(ref, c, z, y=None):
    start = (c * N_Z + z) * N_Y
    if y is None:
        return ref.at[pl.ds(pl.multiple_of(start * BLOCK, 8), N_Y * BLOCK)]
    return ref.at[pl.ds(pl.multiple_of((start + y) * BLOCK, 8), BLOCK)]


class Flow:
    SCRATCH = [
        pltpu.VMEM((N_Z, N_Y * BLOCK, LANES), F32),
        pltpu.VMEM((N_Z, N_Y * BLOCK, LANES), F32),
        pltpu.VMEM((N_Z * (N_Y - 1), BLOCK, LANES), F32),
        pltpu.VMEM((N_Z, BLOCK, LANES), F32),
        pltpu.VMEM((N_Z - 1, BLOCK, LANES), F32),
        pltpu.VMEM((BLOCK, LANES), F32),
        pltpu.VMEM((N_X - 1, BLOCK, LANES), F32),
        pltpu.VMEM((BLOCK, LANES), F32),
        pltpu.VMEM((BLOCK, LANES), F32),
        pltpu.SemaphoreType.DMA((42,)),
        pltpu.SemaphoreType.DMA((42,)),
    ]

    def __init__(self, wires, reverse, local, full, scratch):
        self.w, self.reverse, self.local, self.full = wires, reverse, local, full
        (self.from_core, self.on_chip, self.from_y, self.to_z, self.from_z, self.share, self.from_x,
         self.total, self.from_half, self.sent, self.got) = scratch
        self.column = {k: turn(wires.z, k, N_Z) for k in ORDER}
        self.source = {k: turn(wires.z, -k, N_Z) for k in range(N_Z)}

    def send(self, src, dst, n, peer):
        return self.w.send(src, dst, self.sent.at[n], self.got.at[n], peer)

    def start(self):
        w = self.w
        self.core = {
            k: self.send(block(self.local, 1 - w.c, self.column[k]), self.from_core.at[k], k, w.mate) for k in ORDER
        }

    def over_y(self):
        w = self.w
        self.over = {}
        for k in ORDER:
            self.core[k].wait_recv()
            self.on_chip[k] = block(self.local, w.c, self.column[k])[...] + self.from_core[k]
            for j, peer in enumerate(w.peers_y):
                slot = k * (N_Y - 1) + j
                piece = pl.ds(pl.multiple_of(turn(w.y, j + 1, N_Y) * BLOCK, 8), BLOCK)
                self.over[k, j] = self.send(self.on_chip.at[k, piece], self.from_y.at[slot], 4 + slot, peer)

    def over_z(self):
        w = self.w
        self.line = []
        mine = pl.ds(pl.multiple_of(w.y * BLOCK, 8), BLOCK)
        for k in ORDER:
            value = self.on_chip[k, mine]
            for j in range(N_Y - 1):
                self.over[k, j].wait_recv()
                value = value + self.from_y[k * (N_Y - 1) + j]
            self.to_z[k] = value
            if k:
                self.line.append(self.send(self.to_z.at[k], self.from_z.at[k - 1], 15 + k, w.peers_z[k - 1]))

    def over_x(self):
        value = self.to_z[0]
        for j, copy in enumerate(self.line):
            copy.wait_recv()
            value = value + self.from_z[j]
        self.share[...] = value
        self.rows = [self.send(self.share, self.from_x.at[j], 19 + j, p) for j, p in enumerate(self.w.peers_x)]

    def over_half(self):
        value = self.share[...]
        for j, copy in enumerate(self.rows):
            copy.wait_recv()
            value = value + self.from_x[j]
        self.total[...] = value
        self.cross = self.send(self.total, self.from_half, 22, self.w.other)

    def gather_z(self):
        w = self.w
        value = self.share[...]
        for j in range(N_X - 1):
            wanted = w.x < j + 1 if self.reverse else w.x >= j + 1
            value = value + jnp.where(wanted, self.from_x[j], 0.0)
        self.cross.wait_recv()
        value = value + jnp.where(w.zh == (0 if self.reverse else 1), self.from_half[...], 0.0)
        mine = block(self.full, w.c, w.z, w.y)
        mine[...] = value
        self.spread = {j + 1: self.send(mine, mine, 23 + j, p) for j, p in enumerate(w.peers_z)}
        self.over = {}
        self.gather_y(range(1))

    def gather_y(self, which=range(1, N_Z)):
        w = self.w
        for k in which:
            if k:
                self.spread[k].wait_recv()
            piece = block(self.full, w.c, self.source[k], w.y)
            for j, peer in enumerate(w.peers_y):
                slot = k * (N_Y - 1) + j
                self.over[k, j] = self.send(piece, piece, 26 + slot, peer)

    def gather_core(self):
        w = self.w
        self.last = []
        for k in range(N_Z):
            for j in range(N_Y - 1):
                self.over[k, j].wait_recv()
            piece = block(self.full, w.c, self.source[k])
            self.last.append(self.send(piece, piece, 38 + k, w.mate))

    def finish(self):
        for copy in self.last:
            copy.wait_recv()


class Small:
    SCRATCH = [
        pltpu.VMEM((SMALL, LANES), F32),
        pltpu.VMEM((N_Y * N_C - 1, SMALL, LANES), F32),
        pltpu.VMEM((SMALL, LANES), F32),
        pltpu.VMEM((N_ZH * N_Z - 1, SMALL, LANES), F32),
        pltpu.VMEM((2, SMALL, LANES), F32),
        pltpu.VMEM((N_X - 1, 2, SMALL, LANES), F32),
        pltpu.SemaphoreType.DMA((17,)),
        pltpu.SemaphoreType.DMA((17,)),
    ]

    def __init__(self, wires, reverse, full, scratch):
        self.w, self.reverse, self.full = wires, reverse, full
        self.local, self.from_near, self.near, self.from_ring, self.both, self.from_x, self.sent, self.got = scratch

    def send(self, src, dst, n, peer):
        return self.w.send(src, dst, self.sent.at[n], self.got.at[n], peer)

    def start(self):
        self.copies = [
            self.send(self.local, self.from_near.at[j], j, peer) for j, peer in enumerate(self.w.near)
        ]

    def over_z(self):
        value = self.local[...]
        for j, copy in enumerate(self.copies):
            copy.wait_recv()
            value = value + self.from_near[j]
        self.near[...] = value
        self.copies = [
            self.send(self.near, self.from_ring.at[j], 7 + j, peer) for j, peer in enumerate(self.w.ring)
        ]

    def over_x(self):
        here, there = self.near[...], jnp.zeros((SMALL, LANES), F32)
        for j, copy in enumerate(self.copies):
            copy.wait_recv()
            piece, same = self.from_ring[j], self.w.same_half[j]
            here = here + jnp.where(same, piece, 0.0)
            there = there + jnp.where(same, 0.0, piece)
        self.both[0] = here
        self.both[1] = there
        self.copies = [
            self.send(self.both, self.from_x.at[j], 14 + j, peer) for j, peer in enumerate(self.w.peers_x)
        ]

    def finish(self):
        w = self.w
        value, far = self.both[0], self.both[1]
        for j, copy in enumerate(self.copies):
            copy.wait_recv()
            wanted = w.x < j + 1 if self.reverse else w.x >= j + 1
            value = value + jnp.where(wanted, self.from_x[j, 0], 0.0)
            far = far + self.from_x[j, 1]
        self.full[...] = value + jnp.where(w.zh == (0 if self.reverse else 1), far, 0.0)


N_FLOW, N_SMALL = len(Flow.SCRATCH), len(Small.SCRATCH)


def whole(k_hbm, v_hbm, q_hbm, g_hbm, dq_hbm, r_full, y_full, *scratch):
    k_ref, v_ref, q_ref, g_ref, dq_ref, s_local, r_local, s_full, z_full, inv_ref, io = scratch[:11]
    scratch = scratch[11:]
    loads = [
        pltpu.make_async_copy(src, dst, io.at[n])
        for n, (src, dst) in enumerate([(k_hbm, k_ref), (v_hbm, v_ref), (q_hbm, q_ref), (g_hbm, g_ref)])
    ]
    for load in loads:
        load.start()
    wires = Wires()
    s = Flow(wires, False, s_local, s_full, scratch[:N_FLOW])
    r = Flow(wires, True, r_local, r_full, scratch[N_FLOW : 2 * N_FLOW])
    z = Small(wires, False, z_full, scratch[2 * N_FLOW : 2 * N_FLOW + N_SMALL])
    y = Small(wires, True, y_full, scratch[2 * N_FLOW + N_SMALL :])

    barrier = pltpu.get_barrier_semaphore()
    everyone = [*wires.near, *wires.ring, *wires.peers_x]
    for peer in everyone:
        pl.semaphore_signal(barrier, inc=1, device_id=peer, device_id_type=MESH)

    lane = lax.broadcasted_iota(jnp.int32, (HEAD, LANES), 1)
    loads[0].wait()
    columns = jnp.zeros((HEAD, LANES), F32)
    for h in range(HEADS):
        feat32 = jnp.maximum(k_ref[head_rows(h), :], 0).astype(F32)
        columns = jnp.where(lane == h, lane_sums(feat32), columns)
    z.local[...] = as_rows(columns)
    pl.semaphore_wait(barrier, len(everyone))
    z.start()

    loads[1].wait()
    for h in range(HEADS):
        rows = head_rows(h)
        s_local[rows, :] = dot(jnp.maximum(k_ref[rows, :], 0), under(v_ref[rows, :], 1.0), (1, 1))
    s_local[HEADS * HEAD :, :] = jnp.zeros((ROWS - HEADS * HEAD, LANES), F32)
    s.start()
    r_local[...] = jnp.zeros((ROWS, LANES), F32)
    s.over_y()
    z.over_z()
    z.over_x()
    s.over_z()
    loads[2].wait()
    loads[3].wait()
    z.finish()

    norms = z_full[...].T[:HEAD]
    for h in range(HEADS):
        rows = head_rows(h)
        feat32 = jnp.maximum(q_ref[rows, :], 0).astype(F32)
        inv = 1.0 / (jnp.sum(feat32 * norms[:, h : h + 1], axis=0, keepdims=True) + 1.0)
        inv_ref[h : h + 1, :] = inv
        pair = dot(jnp.concatenate(halves(feat32 * inv), 0), g_ref[rows, :], (1, 1))
        r_local[rows, :HEAD] = pair[:HEAD] + pair[HEAD:]
    r.start()
    s.over_x()
    r.over_y()
    s.over_half()
    s.gather_z()
    r.over_z()
    s.gather_y()
    r.over_x()
    r.over_half()
    s.gather_core()
    s.finish()

    columns = jnp.zeros((HEAD, LANES), F32)
    for h in range(HEADS):
        rows = head_rows(h)
        feat32 = jnp.maximum(q_ref[rows, :], 0).astype(F32)
        inv = inv_ref[h : h + 1, :]
        state = s_full[rows, :]
        pair = dot(jnp.concatenate(halves(state[:, :HEAD]), 0), g_ref[rows, :], (1, 0))
        back = pair[:HEAD] + pair[HEAD:]
        along = jnp.sum(feat32 * back, axis=0, keepdims=True)
        grad_den = -(along * inv) * inv
        norm = state[:, HEAD : HEAD + 1]
        dq_ref[rows, :] = jnp.where(feat32 > 0, back * inv + norm * grad_den, 0.0).astype(BF16)
        columns = jnp.where(lane == h, lane_sums(feat32 * grad_den), columns)
    y.local[...] = as_rows(columns)
    y.start()
    out = pltpu.make_async_copy(dq_ref, dq_hbm, io.at[4])
    out.start()
    r.gather_z()
    r.gather_y()
    y.over_z()
    y.over_x()
    r.gather_core()
    r.finish()
    y.finish()
    out.wait()
    for copy in wires.started:
        copy.wait_send()


def key_side(k_ref, v_ref, r_ref, y_ref, dk_hbm, dv_hbm, dk_ref, dv_ref, io):
    norms = y_ref[...].T[:HEAD]
    copies = []
    for h in range(HEADS):
        rows = head_rows(h)
        feat = jnp.maximum(k_ref[rows, :], 0)
        state = r_ref[rows, :]
        pair = dot(jnp.concatenate(halves(state), 1), feat, (0, 0))
        dv_ref[rows, :] = (pair[:HEAD] + pair[LANES : LANES + HEAD]).astype(BF16)
        pair = dot(jnp.concatenate(halves(state[:, :HEAD]), 0), v_ref[rows, :], (1, 0))
        grad_k = pair[:HEAD] + pair[HEAD:] + norms[:, h : h + 1]
        dk_ref[rows, :] = jnp.where(feat.astype(F32) > 0, grad_k, 0.0).astype(BF16)
        if h % GROUP == GROUP - 1:
            done = pl.ds(HEAD * (h + 1 - GROUP), HEAD * GROUP)
            for src, dst in ((dk_ref, dk_hbm), (dv_ref, dv_hbm)):
                copies.append(pltpu.make_async_copy(src.at[done], dst.at[done], io.at[len(copies)]))
                copies[-1].start()
    for copy in copies:
        copy.wait()


def on_device(queries, keys, values, out_grad):
    queries, keys, values, out_grad = queries.T, keys.T, values.T, out_grad.T
    width, tokens = queries.shape
    like = jax.ShapeDtypeStruct((width, tokens), BF16)
    anywhere = pl.BlockSpec(memory_space=pl.ANY)
    hbm = pl.BlockSpec(memory_space=pltpu.HBM)
    vmem = pl.BlockSpec(memory_space=pltpu.VMEM)
    query_grad, r_full, y_full = pl.pallas_call(
        whole,
        out_shape=(like, jax.ShapeDtypeStruct((ROWS, LANES), F32), jax.ShapeDtypeStruct((SMALL, LANES), F32)),
        in_specs=[hbm] * 4,
        out_specs=(anywhere, vmem, vmem),
        scratch_shapes=[
            *[pltpu.VMEM((width, tokens), BF16)] * 5,
            *[pltpu.VMEM((ROWS, LANES), F32)] * 3,
            pltpu.VMEM((SMALL, LANES), F32),
            pltpu.VMEM((SMALL, tokens), F32),
            pltpu.SemaphoreType.DMA((5,)),
            *Flow.SCRATCH, *Flow.SCRATCH, *Small.SCRATCH, *Small.SCRATCH,
        ],
        compiler_params=pltpu.CompilerParams(
            collective_id=0, has_side_effects=True, vmem_limit_bytes=WHOLE_VMEM
        ),
        name="whole",
    )(*[pltpu.with_memory_space_constraint(a, pltpu.HBM) for a in (keys, values, queries, out_grad)])
    key_grad, value_grad = pl.pallas_call(
        key_side,
        out_shape=(like, like),
        in_specs=[vmem] * 4,
        out_specs=(anywhere, anywhere),
        scratch_shapes=[
            *[pltpu.VMEM((width, tokens), BF16)] * 2,
            pltpu.SemaphoreType.DMA((2 * HEADS // GROUP,)),
        ],
        name="key_side",
        compiler_params=pltpu.CompilerParams(vmem_limit_bytes=LAST_VMEM),
    )(keys, values, r_full, y_full)
    return query_grad.T, key_grad.T, value_grad.T


def solution(mesh):
    spec = P(("tm", "space"), None)
    return jax.shard_map(
        on_device, mesh=mesh, in_specs=(spec,) * 4, out_specs=(spec,) * 3, check_vma=False
    )
```

```python
import functools

import jax
import jax.numpy as jnp
from jax import lax
from jax.experimental import pallas as pl
from jax.experimental.pallas import tpu as pltpu
from jax.sharding import PartitionSpec as P

HEADS = 20
HEAD = 112
LANES = 128
N_X, N_ZH, N_Z, N_Y, N_C = 4, 2, 4, 4, 2
BLOCK = 8 * -(-HEADS * HEAD // (8 * N_Z * N_Y * N_C))
ROWS = BLOCK * N_Z * N_Y * N_C
SMALL = 8 * -(-HEADS // 8)
GROUP = 4
WHOLE_VMEM = 26 * 1024 * 1024
LAST_VMEM = 24 * 1024 * 1024
MESH = pl.DeviceIdType.MESH
F32, BF16 = jnp.float32, jnp.bfloat16
ORDER = [*range(1, N_Z), 0]


def halves(x):
    high = x.astype(BF16)
    low = (x - high.astype(F32)).astype(BF16)
    return high, low


def dot(a, b, contract):
    return lax.dot_general(a, b, ((contract[:1], contract[1:]), ((), ())), preferred_element_type=F32)


def head_rows(h):
    return slice(HEAD * h, HEAD * (h + 1))


def under(rows, first):
    rest = jnp.zeros((LANES - HEAD, rows.shape[1]), F32)
    at = lax.broadcasted_iota(jnp.int32, rest.shape, 0)
    return jnp.concatenate([rows, jnp.where(at == 0, first, rest).astype(rows.dtype)], 0)


def lane_sums(x):
    parts = [x[:, at : at + LANES] for at in range(0, x.shape[1], LANES)]
    return jnp.sum(sum(parts[1:], parts[0]), axis=1, keepdims=True)


def as_rows(columns):
    blank = jnp.zeros((LANES - HEAD, LANES), F32)
    return jnp.concatenate([columns, blank], 0).T[:SMALL]


def turn(v, k, n):
    return lax.rem(v + (k + n), n)


class Wires:
    def __init__(self):
        tm, space = lax.axis_index("tm"), lax.axis_index("space")
        self.zh, self.x = lax.div(tm, N_X), lax.rem(tm, N_X)
        self.z, rest = lax.div(space, N_Y * N_C), lax.rem(space, N_Y * N_C)
        self.y, self.c = lax.div(rest, N_C), lax.rem(rest, N_C)
        self.started = []
        self.mate = self.at(c=1 - self.c)
        self.other = self.at(zh=1 - self.zh)
        self.peers_y = [self.at(y=turn(self.y, j, N_Y)) for j in range(1, N_Y)]
        self.peers_z = [self.at(z=turn(self.z, j, N_Z)) for j in range(1, N_Z)]
        self.peers_x = [self.at(x=turn(self.x, j, N_X)) for j in range(1, N_X)]
        self.near = [
            self.at(y=turn(self.y, j, N_Y), c=turn(self.c, i, N_C))
            for j in range(N_Y) for i in range(N_C) if i or j
        ]
        depth = self.zh * N_Z + self.z
        self.ring = []
        for k in range(1, N_ZH * N_Z):
            d = turn(depth, k, N_ZH * N_Z)
            self.ring.append(self.at(zh=lax.div(d, N_Z), z=lax.rem(d, N_Z)))
        self.same_half = [
            lax.div(turn(depth, -k, N_ZH * N_Z), N_Z) == self.zh for k in range(1, N_ZH * N_Z)
        ]

    def at(self, **moved):
        zh, x, z, y, c = (moved.get(n, getattr(self, n, None)) for n in ("zh", "x", "z", "y", "c"))
        return (zh * N_X + x, (z * N_Y + y) * N_C + c)

    def send(self, src, dst, send_sem, recv_sem, peer):
        copy = pltpu.make_async_remote_copy(
            src_ref=src, dst_ref=dst, send_sem=send_sem, recv_sem=recv_sem, device_id=peer, device_id_type=MESH
        )
        copy.start()
        self.started.append(copy)
        return copy


def block(ref, c, z, y=None):
    start = (c * N_Z + z) * N_Y
    if y is None:
        return ref.at[pl.ds(pl.multiple_of(start * BLOCK, 8), N_Y * BLOCK)]
    return ref.at[pl.ds(pl.multiple_of((start + y) * BLOCK, 8), BLOCK)]


class Flow:
    SCRATCH = [
        pltpu.VMEM((N_Z, N_Y * BLOCK, LANES), F32),
        pltpu.VMEM((N_Z, N_Y * BLOCK, LANES), F32),
        pltpu.VMEM((N_Z * (N_Y - 1), BLOCK, LANES), F32),
        pltpu.VMEM((N_Z, BLOCK, LANES), F32),
        pltpu.VMEM((N_Z - 1, BLOCK, LANES), F32),
        pltpu.VMEM((BLOCK, LANES), F32),
        pltpu.VMEM((N_X - 1, BLOCK, LANES), F32),
        pltpu.VMEM((BLOCK, LANES), F32),
        pltpu.VMEM((BLOCK, LANES), F32),
        pltpu.SemaphoreType.DMA((42,)),
        pltpu.SemaphoreType.DMA((42,)),
    ]

    def __init__(self, wires, reverse, local, full, scratch):
        self.w, self.reverse, self.local, self.full = wires, reverse, local, full
        (self.from_core, self.on_chip, self.from_y, self.to_z, self.from_z, self.share, self.from_x,
         self.total, self.from_half, self.sent, self.got) = scratch
        self.column = {k: turn(wires.z, k, N_Z) for k in ORDER}
        self.source = {k: turn(wires.z, -k, N_Z) for k in range(N_Z)}

    def send(self, src, dst, n, peer):
        return self.w.send(src, dst, self.sent.at[n], self.got.at[n], peer)

    def start(self):
        w = self.w
        self.core = {
            k: self.send(block(self.local, 1 - w.c, self.column[k]), self.from_core.at[k], k, w.mate) for k in ORDER
        }

    def over_y(self):
        w = self.w
        self.over = {}
        for k in ORDER:
            self.core[k].wait_recv()
            self.on_chip[k] = block(self.local, w.c, self.column[k])[...] + self.from_core[k]
            for j, peer in enumerate(w.peers_y):
                slot = k * (N_Y - 1) + j
                piece = pl.ds(pl.multiple_of(turn(w.y, j + 1, N_Y) * BLOCK, 8), BLOCK)
                self.over[k, j] = self.send(self.on_chip.at[k, piece], self.from_y.at[slot], 4 + slot, peer)

    def over_z(self):
        w = self.w
        self.line = []
        mine = pl.ds(pl.multiple_of(w.y * BLOCK, 8), BLOCK)
        for k in ORDER:
            value = self.on_chip[k, mine]
            for j in range(N_Y - 1):
                self.over[k, j].wait_recv()
                value = value + self.from_y[k * (N_Y - 1) + j]
            self.to_z[k] = value
            if k:
                self.line.append(self.send(self.to_z.at[k], self.from_z.at[k - 1], 15 + k, w.peers_z[k - 1]))

    def over_x(self):
        value = self.to_z[0]
        for j, copy in enumerate(self.line):
            copy.wait_recv()
            value = value + self.from_z[j]
        self.share[...] = value
        self.rows = [self.send(self.share, self.from_x.at[j], 19 + j, p) for j, p in enumerate(self.w.peers_x)]

    def over_half(self):
        value = self.share[...]
        for j, copy in enumerate(self.rows):
            copy.wait_recv()
            value = value + self.from_x[j]
        self.total[...] = value
        self.cross = self.send(self.total, self.from_half, 22, self.w.other)

    def gather_z(self):
        w = self.w
        value = self.share[...]
        for j in range(N_X - 1):
            wanted = w.x < j + 1 if self.reverse else w.x >= j + 1
            value = value + jnp.where(wanted, self.from_x[j], 0.0)
        self.cross.wait_recv()
        value = value + jnp.where(w.zh == (0 if self.reverse else 1), self.from_half[...], 0.0)
        mine = block(self.full, w.c, w.z, w.y)
        mine[...] = value
        self.spread = {j + 1: self.send(mine, mine, 23 + j, p) for j, p in enumerate(w.peers_z)}
        self.over = {}
        self.gather_y(range(1))

    def gather_y(self, which=range(1, N_Z)):
        w = self.w
        for k in which:
            if k:
                self.spread[k].wait_recv()
            piece = block(self.full, w.c, self.source[k], w.y)
            for j, peer in enumerate(w.peers_y):
                slot = k * (N_Y - 1) + j
                self.over[k, j] = self.send(piece, piece, 26 + slot, peer)

    def gather_core(self):
        w = self.w
        self.last = []
        for k in range(N_Z):
            for j in range(N_Y - 1):
                self.over[k, j].wait_recv()
            piece = block(self.full, w.c, self.source[k])
            self.last.append(self.send(piece, piece, 38 + k, w.mate))

    def finish(self):
        for copy in self.last:
            copy.wait_recv()


class Small:
    SCRATCH = [
        pltpu.VMEM((SMALL, LANES), F32),
        pltpu.VMEM((N_Y * N_C - 1, SMALL, LANES), F32),
        pltpu.VMEM((SMALL, LANES), F32),
        pltpu.VMEM((N_ZH * N_Z - 1, SMALL, LANES), F32),
        pltpu.VMEM((2, SMALL, LANES), F32),
        pltpu.VMEM((N_X - 1, 2, SMALL, LANES), F32),
        pltpu.SemaphoreType.DMA((17,)),
        pltpu.SemaphoreType.DMA((17,)),
    ]

    def __init__(self, wires, reverse, full, scratch):
        self.w, self.reverse, self.full = wires, reverse, full
        self.local, self.from_near, self.near, self.from_ring, self.both, self.from_x, self.sent, self.got = scratch

    def send(self, src, dst, n, peer):
        return self.w.send(src, dst, self.sent.at[n], self.got.at[n], peer)

    def start(self):
        self.copies = [
            self.send(self.local, self.from_near.at[j], j, peer) for j, peer in enumerate(self.w.near)
        ]

    def over_z(self):
        value = self.local[...]
        for j, copy in enumerate(self.copies):
            copy.wait_recv()
            value = value + self.from_near[j]
        self.near[...] = value
        self.copies = [
            self.send(self.near, self.from_ring.at[j], 7 + j, peer) for j, peer in enumerate(self.w.ring)
        ]

    def over_x(self):
        here, there = self.near[...], jnp.zeros((SMALL, LANES), F32)
        for j, copy in enumerate(self.copies):
            copy.wait_recv()
            piece, same = self.from_ring[j], self.w.same_half[j]
            here = here + jnp.where(same, piece, 0.0)
            there = there + jnp.where(same, 0.0, piece)
        self.both[0] = here
        self.both[1] = there
        self.copies = [
            self.send(self.both, self.from_x.at[j], 14 + j, peer) for j, peer in enumerate(self.w.peers_x)
        ]

    def finish(self):
        w = self.w
        value, far = self.both[0], self.both[1]
        for j, copy in enumerate(self.copies):
            copy.wait_recv()
            wanted = w.x < j + 1 if self.reverse else w.x >= j + 1
            value = value + jnp.where(wanted, self.from_x[j, 0], 0.0)
            far = far + self.from_x[j, 1]
        self.full[...] = value + jnp.where(w.zh == (0 if self.reverse else 1), far, 0.0)


N_FLOW, N_SMALL = len(Flow.SCRATCH), len(Small.SCRATCH)


def whole(k_hbm, v_hbm, q_hbm, g_hbm, dq_ref, r_full, y_full, *scratch):
    k_ref, v_ref, q_ref, g_ref, s_local, r_local, s_full, z_full, inv_ref, io = scratch[:10]
    scratch = scratch[10:]
    loads = [
        pltpu.make_async_copy(src, dst, io.at[n])
        for n, (src, dst) in enumerate([(k_hbm, k_ref), (v_hbm, v_ref), (q_hbm, q_ref), (g_hbm, g_ref)])
    ]
    for load in loads[:2]:
        load.start()
    wires = Wires()
    s = Flow(wires, False, s_local, s_full, scratch[:N_FLOW])
    r = Flow(wires, True, r_local, r_full, scratch[N_FLOW : 2 * N_FLOW])
    z = Small(wires, False, z_full, scratch[2 * N_FLOW : 2 * N_FLOW + N_SMALL])
    y = Small(wires, True, y_full, scratch[2 * N_FLOW + N_SMALL :])

    barrier = pltpu.get_barrier_semaphore()
    everyone = [*wires.near, *wires.ring, *wires.peers_x]
    for peer in everyone:
        pl.semaphore_signal(barrier, inc=1, device_id=peer, device_id_type=MESH)

    lane = lax.broadcasted_iota(jnp.int32, (HEAD, LANES), 1)
    loads[0].wait()
    columns = jnp.zeros((HEAD, LANES), F32)
    for h in range(HEADS):
        feat32 = jnp.maximum(k_ref[head_rows(h), :], 0).astype(F32)
        columns = jnp.where(lane == h, lane_sums(feat32), columns)
    z.local[...] = as_rows(columns)
    pl.semaphore_wait(barrier, len(everyone))
    z.start()
    for load in loads[2:]:
        load.start()

    loads[1].wait()
    for h in range(HEADS):
        rows = head_rows(h)
        s_local[rows, :] = dot(jnp.maximum(k_ref[rows, :], 0), under(v_ref[rows, :], 1.0), (1, 1))
    s_local[HEADS * HEAD :, :] = jnp.zeros((ROWS - HEADS * HEAD, LANES), F32)
    s.start()
    r_local[...] = jnp.zeros((ROWS, LANES), F32)
    s.over_y()
    z.over_z()
    z.over_x()
    s.over_z()
    loads[2].wait()
    loads[3].wait()
    z.finish()

    norms = z_full[...].T[:HEAD]
    for h in range(HEADS):
        rows = head_rows(h)
        feat32 = jnp.maximum(q_ref[rows, :], 0).astype(F32)
        inv = 1.0 / (jnp.sum(feat32 * norms[:, h : h + 1], axis=0, keepdims=True) + 1.0)
        inv_ref[h : h + 1, :] = inv
        pair = dot(jnp.concatenate(halves(feat32 * inv), 0), g_ref[rows, :], (1, 1))
        r_local[rows, :HEAD] = pair[:HEAD] + pair[HEAD:]
    r.start()
    s.over_x()
    r.over_y()
    s.over_half()
    s.gather_z()
    r.over_z()
    r.over_x()
    s.gather_y()
    r.over_half()
    s.gather_core()

    def query_heads(first, count, columns):
        for n in range(count):
            h = first + n
            rows = pl.ds(pl.multiple_of(h * HEAD, 16), HEAD)
            feat32 = jnp.maximum(q_ref[rows, :], 0).astype(F32)
            inv = inv_ref[pl.ds(h, 1), :]
            state = s_full[rows, :]
            pair = dot(jnp.concatenate(halves(state[:, :HEAD]), 0), g_ref[rows, :], (1, 0))
            back = pair[:HEAD] + pair[HEAD:]
            along = jnp.sum(feat32 * back, axis=0, keepdims=True)
            grad_den = -(along * inv) * inv
            norm = state[:, HEAD : HEAD + 1]
            dq_ref[rows, :] = jnp.where(feat32 > 0, back * inv + norm * grad_den, 0.0).astype(BF16)
            columns = jnp.where(lane == h, lane_sums(feat32 * grad_den), columns)
        return columns

    early = ROWS // N_C // HEAD - 1
    columns = query_heads(wires.c * (HEADS - early), early, jnp.zeros((HEAD, LANES), F32))
    r.gather_z()
    s.finish()
    columns = query_heads((1 - wires.c) * early, HEADS - early, columns)
    y.local[...] = as_rows(columns)
    y.start()
    r.gather_y()
    y.over_z()
    y.over_x()
    r.gather_core()
    r.finish()
    y.finish()
    for copy in wires.started:
        copy.wait_send()


def key_side(k_ref, v_ref, r_ref, y_ref, dq_ref, dk_hbm, dv_hbm, dq_hbm, dk_ref, dv_ref, io):
    norms = y_ref[...].T[:HEAD]
    copies = [pltpu.make_async_copy(dq_ref, dq_hbm, io.at[0])]
    copies[0].start()
    for h in range(HEADS):
        rows = head_rows(h)
        feat = jnp.maximum(k_ref[rows, :], 0)
        state = r_ref[rows, :]
        pair = dot(jnp.concatenate(halves(state), 1), feat, (0, 0))
        dv_ref[rows, :] = (pair[:HEAD] + pair[LANES : LANES + HEAD]).astype(BF16)
        pair = dot(jnp.concatenate(halves(state[:, :HEAD]), 0), v_ref[rows, :], (1, 0))
        grad_k = pair[:HEAD] + pair[HEAD:] + norms[:, h : h + 1]
        dk_ref[rows, :] = jnp.where(feat.astype(F32) > 0, grad_k, 0.0).astype(BF16)
        if h % GROUP == GROUP - 1:
            done = pl.ds(HEAD * (h + 1 - GROUP), HEAD * GROUP)
            for src, dst in ((dk_ref, dk_hbm), (dv_ref, dv_hbm)):
                copies.append(pltpu.make_async_copy(src.at[done], dst.at[done], io.at[len(copies)]))
                copies[-1].start()
    for copy in copies:
        copy.wait()


def on_device(queries, keys, values, out_grad):
    queries, keys, values, out_grad = queries.T, keys.T, values.T, out_grad.T
    width, tokens = queries.shape
    like = jax.ShapeDtypeStruct((width, tokens), BF16)
    anywhere = pl.BlockSpec(memory_space=pl.ANY)
    hbm = pl.BlockSpec(memory_space=pltpu.HBM)
    vmem = pl.BlockSpec(memory_space=pltpu.VMEM)
    query_grad, r_full, y_full = pl.pallas_call(
        whole,
        out_shape=(like, jax.ShapeDtypeStruct((ROWS, LANES), F32), jax.ShapeDtypeStruct((SMALL, LANES), F32)),
        in_specs=[hbm] * 4,
        out_specs=(vmem, vmem, vmem),
        scratch_shapes=[
            *[pltpu.VMEM((width, tokens), BF16)] * 4,
            *[pltpu.VMEM((ROWS, LANES), F32)] * 3,
            pltpu.VMEM((SMALL, LANES), F32),
            pltpu.VMEM((SMALL, tokens), F32),
            pltpu.SemaphoreType.DMA((4,)),
            *Flow.SCRATCH, *Flow.SCRATCH, *Small.SCRATCH, *Small.SCRATCH,
        ],
        compiler_params=pltpu.CompilerParams(
            collective_id=0, has_side_effects=True, vmem_limit_bytes=WHOLE_VMEM
        ),
        name="whole",
    )(*[pltpu.with_memory_space_constraint(a, pltpu.HBM) for a in (keys, values, queries, out_grad)])
    key_grad, value_grad, query_grad = pl.pallas_call(
        key_side,
        out_shape=(like, like, like),
        in_specs=[vmem] * 5,
        out_specs=(anywhere, anywhere, anywhere),
        scratch_shapes=[
            *[pltpu.VMEM((width, tokens), BF16)] * 2,
            pltpu.SemaphoreType.DMA((1 + 2 * HEADS // GROUP,)),
        ],
        name="key_side",
        compiler_params=pltpu.CompilerParams(vmem_limit_bytes=LAST_VMEM),
    )(keys, values, r_full, y_full, query_grad)
    return query_grad.T, key_grad.T, value_grad.T


def solution(mesh):
    spec = P(("tm", "space"), None)
    return jax.shard_map(
        on_device, mesh=mesh, in_specs=(spec,) * 4, out_specs=(spec,) * 3, check_vma=False
    )
```

```python
import functools

import jax
import jax.numpy as jnp
from jax import lax
from jax.experimental import pallas as pl
from jax.experimental.pallas import tpu as pltpu
from jax.sharding import PartitionSpec as P

HEADS = 20
HEAD = 112
LANES = 128
N_X, N_ZH, N_Z, N_Y, N_C = 4, 2, 4, 4, 2
BLOCK = 8 * -(-HEADS * HEAD // (8 * N_Z * N_Y * N_C))
ROWS = BLOCK * N_Z * N_Y * N_C
SMALL = 8 * -(-HEADS // 8)
GROUP = 4
WHOLE_VMEM = 26 * 1024 * 1024
LAST_VMEM = 24 * 1024 * 1024
MESH = pl.DeviceIdType.MESH
F32, BF16 = jnp.float32, jnp.bfloat16
ORDER = [*range(1, N_Z), 0]


def halves(x):
    high = x.astype(BF16)
    low = (x - high.astype(F32)).astype(BF16)
    return high, low


def dot(a, b, contract):
    return lax.dot_general(a, b, ((contract[:1], contract[1:]), ((), ())), preferred_element_type=F32)


def head_rows(h):
    return slice(HEAD * h, HEAD * (h + 1))


def under(rows, first):
    rest = jnp.zeros((LANES - HEAD, rows.shape[1]), F32)
    at = lax.broadcasted_iota(jnp.int32, rest.shape, 0)
    return jnp.concatenate([rows, jnp.where(at == 0, first, rest).astype(rows.dtype)], 0)


def lane_sums(x):
    parts = [x[:, at : at + LANES] for at in range(0, x.shape[1], LANES)]
    return jnp.sum(sum(parts[1:], parts[0]), axis=1, keepdims=True)


def as_rows(columns):
    blank = jnp.zeros((LANES - HEAD, LANES), F32)
    return jnp.concatenate([columns, blank], 0).T[:SMALL]


def turn(v, k, n):
    return lax.rem(v + (k + n), n)


class Wires:
    def __init__(self):
        tm, space = lax.axis_index("tm"), lax.axis_index("space")
        self.zh, self.x = lax.div(tm, N_X), lax.rem(tm, N_X)
        self.z, rest = lax.div(space, N_Y * N_C), lax.rem(space, N_Y * N_C)
        self.y, self.c = lax.div(rest, N_C), lax.rem(rest, N_C)
        self.started = []
        self.mate = self.at(c=1 - self.c)
        self.other = self.at(zh=1 - self.zh)
        self.peers_y = [self.at(y=turn(self.y, j, N_Y)) for j in range(1, N_Y)]
        self.peers_z = [self.at(z=turn(self.z, j, N_Z)) for j in range(1, N_Z)]
        self.peers_x = [self.at(x=turn(self.x, j, N_X)) for j in range(1, N_X)]
        self.near = [
            self.at(y=turn(self.y, j, N_Y), c=turn(self.c, i, N_C))
            for j in range(N_Y) for i in range(N_C) if i or j
        ]
        depth = self.zh * N_Z + self.z
        self.ring = []
        for k in range(1, N_ZH * N_Z):
            d = turn(depth, k, N_ZH * N_Z)
            self.ring.append(self.at(zh=lax.div(d, N_Z), z=lax.rem(d, N_Z)))
        self.same_half = [
            lax.div(turn(depth, -k, N_ZH * N_Z), N_Z) == self.zh for k in range(1, N_ZH * N_Z)
        ]

    def at(self, **moved):
        zh, x, z, y, c = (moved.get(n, getattr(self, n, None)) for n in ("zh", "x", "z", "y", "c"))
        return (zh * N_X + x, (z * N_Y + y) * N_C + c)

    def send(self, src, dst, send_sem, recv_sem, peer):
        copy = pltpu.make_async_remote_copy(
            src_ref=src, dst_ref=dst, send_sem=send_sem, recv_sem=recv_sem, device_id=peer, device_id_type=MESH
        )
        copy.start()
        self.started.append(copy)
        return copy


def block(ref, c, z, y=None):
    start = (c * N_Z + z) * N_Y
    if y is None:
        return ref.at[pl.ds(pl.multiple_of(start * BLOCK, 8), N_Y * BLOCK)]
    return ref.at[pl.ds(pl.multiple_of((start + y) * BLOCK, 8), BLOCK)]


class Flow:
    SCRATCH = [
        pltpu.VMEM((N_Z, N_Y * BLOCK, LANES), F32),
        pltpu.VMEM((N_Z, N_Y * BLOCK, LANES), F32),
        pltpu.VMEM((N_Z * (N_Y - 1), BLOCK, LANES), F32),
        pltpu.VMEM((N_Z, BLOCK, LANES), F32),
        pltpu.VMEM((N_Z - 1, BLOCK, LANES), F32),
        pltpu.VMEM((BLOCK, LANES), F32),
        pltpu.VMEM((N_X - 1, BLOCK, LANES), F32),
        pltpu.VMEM((BLOCK, LANES), F32),
        pltpu.VMEM((BLOCK, LANES), F32),
        pltpu.SemaphoreType.DMA((42,)),
        pltpu.SemaphoreType.DMA((42,)),
    ]

    def __init__(self, wires, reverse, local, full, scratch):
        self.w, self.reverse, self.local, self.full = wires, reverse, local, full
        (self.from_core, self.on_chip, self.from_y, self.to_z, self.from_z, self.share, self.from_x,
         self.total, self.from_half, self.sent, self.got) = scratch
        self.column = {k: turn(wires.z, k, N_Z) for k in ORDER}
        self.source = {k: turn(wires.z, -k, N_Z) for k in range(N_Z)}

    def send(self, src, dst, n, peer):
        return self.w.send(src, dst, self.sent.at[n], self.got.at[n], peer)

    def start(self):
        w = self.w
        self.core = {
            k: self.send(block(self.local, 1 - w.c, self.column[k]), self.from_core.at[k], k, w.mate) for k in ORDER
        }

    def over_y(self):
        w = self.w
        self.over = {}
        for k in ORDER:
            self.core[k].wait_recv()
            self.on_chip[k] = block(self.local, w.c, self.column[k])[...] + self.from_core[k]
            for j, peer in enumerate(w.peers_y):
                slot = k * (N_Y - 1) + j
                piece = pl.ds(pl.multiple_of(turn(w.y, j + 1, N_Y) * BLOCK, 8), BLOCK)
                self.over[k, j] = self.send(self.on_chip.at[k, piece], self.from_y.at[slot], 4 + slot, peer)

    def over_z(self):
        w = self.w
        self.line = []
        mine = pl.ds(pl.multiple_of(w.y * BLOCK, 8), BLOCK)
        for k in ORDER:
            value = self.on_chip[k, mine]
            for j in range(N_Y - 1):
                self.over[k, j].wait_recv()
                value = value + self.from_y[k * (N_Y - 1) + j]
            self.to_z[k] = value
            if k:
                self.line.append(self.send(self.to_z.at[k], self.from_z.at[k - 1], 15 + k, w.peers_z[k - 1]))

    def over_x(self):
        value = self.to_z[0]
        for j, copy in enumerate(self.line):
            copy.wait_recv()
            value = value + self.from_z[j]
        self.share[...] = value
        self.rows = [self.send(self.share, self.from_x.at[j], 19 + j, p) for j, p in enumerate(self.w.peers_x)]

    def over_half(self):
        value = self.share[...]
        for j, copy in enumerate(self.rows):
            copy.wait_recv()
            value = value + self.from_x[j]
        self.total[...] = value
        self.cross = self.send(self.total, self.from_half, 22, self.w.other)

    def gather_z(self):
        w = self.w
        value = self.share[...]
        for j in range(N_X - 1):
            wanted = w.x < j + 1 if self.reverse else w.x >= j + 1
            value = value + jnp.where(wanted, self.from_x[j], 0.0)
        self.cross.wait_recv()
        value = value + jnp.where(w.zh == (0 if self.reverse else 1), self.from_half[...], 0.0)
        mine = block(self.full, w.c, w.z, w.y)
        mine[...] = value
        self.spread = {j + 1: self.send(mine, mine, 23 + j, p) for j, p in enumerate(w.peers_z)}
        self.over = {}
        self.gather_y(range(1))

    def gather_y(self, which=range(1, N_Z)):
        w = self.w
        for k in which:
            if k:
                self.spread[k].wait_recv()
            piece = block(self.full, w.c, self.source[k], w.y)
            for j, peer in enumerate(w.peers_y):
                slot = k * (N_Y - 1) + j
                self.over[k, j] = self.send(piece, piece, 26 + slot, peer)

    def gather_core(self):
        w = self.w
        self.last = []
        for k in range(N_Z):
            for j in range(N_Y - 1):
                self.over[k, j].wait_recv()
            piece = block(self.full, w.c, self.source[k])
            self.last.append(self.send(piece, piece, 38 + k, w.mate))

    def finish(self):
        for copy in self.last:
            copy.wait_recv()


class Small:
    SCRATCH = [
        pltpu.VMEM((SMALL, LANES), F32),
        pltpu.VMEM((N_Y * N_C - 1, SMALL, LANES), F32),
        pltpu.VMEM((SMALL, LANES), F32),
        pltpu.VMEM((N_ZH * N_Z - 1, SMALL, LANES), F32),
        pltpu.VMEM((2, SMALL, LANES), F32),
        pltpu.VMEM((N_X - 1, 2, SMALL, LANES), F32),
        pltpu.SemaphoreType.DMA((17,)),
        pltpu.SemaphoreType.DMA((17,)),
    ]

    def __init__(self, wires, reverse, full, scratch):
        self.w, self.reverse, self.full = wires, reverse, full
        self.local, self.from_near, self.near, self.from_ring, self.both, self.from_x, self.sent, self.got = scratch

    def send(self, src, dst, n, peer):
        return self.w.send(src, dst, self.sent.at[n], self.got.at[n], peer)

    def start(self):
        self.copies = [
            self.send(self.local, self.from_near.at[j], j, peer) for j, peer in enumerate(self.w.near)
        ]

    def over_z(self):
        value = self.local[...]
        for j, copy in enumerate(self.copies):
            copy.wait_recv()
            value = value + self.from_near[j]
        self.near[...] = value
        self.copies = [
            self.send(self.near, self.from_ring.at[j], 7 + j, peer) for j, peer in enumerate(self.w.ring)
        ]

    def over_x(self):
        here, there = self.near[...], jnp.zeros((SMALL, LANES), F32)
        for j, copy in enumerate(self.copies):
            copy.wait_recv()
            piece, same = self.from_ring[j], self.w.same_half[j]
            here = here + jnp.where(same, piece, 0.0)
            there = there + jnp.where(same, 0.0, piece)
        self.both[0] = here
        self.both[1] = there
        self.copies = [
            self.send(self.both, self.from_x.at[j], 14 + j, peer) for j, peer in enumerate(self.w.peers_x)
        ]

    def finish(self):
        w = self.w
        value, far = self.both[0], self.both[1]
        for j, copy in enumerate(self.copies):
            copy.wait_recv()
            wanted = w.x < j + 1 if self.reverse else w.x >= j + 1
            value = value + jnp.where(wanted, self.from_x[j, 0], 0.0)
            far = far + self.from_x[j, 1]
        self.full[...] = value + jnp.where(w.zh == (0 if self.reverse else 1), far, 0.0)


N_FLOW, N_SMALL = len(Flow.SCRATCH), len(Small.SCRATCH)


def whole(k_hbm, v_hbm, q_hbm, g_hbm, dq_ref, r_full, y_full, *scratch):
    k_ref, v_ref, q_ref, g_ref, s_local, r_local, s_full, z_full, inv_ref, io = scratch[:10]
    scratch = scratch[10:]
    loads = [
        pltpu.make_async_copy(src, dst, io.at[n])
        for n, (src, dst) in enumerate([(k_hbm, k_ref), (v_hbm, v_ref), (q_hbm, q_ref), (g_hbm, g_ref)])
    ]
    for load in loads:
        load.start()
    wires = Wires()
    s = Flow(wires, False, s_local, s_full, scratch[:N_FLOW])
    r = Flow(wires, True, r_local, r_full, scratch[N_FLOW : 2 * N_FLOW])
    z = Small(wires, False, z_full, scratch[2 * N_FLOW : 2 * N_FLOW + N_SMALL])
    y = Small(wires, True, y_full, scratch[2 * N_FLOW + N_SMALL :])

    barrier = pltpu.get_barrier_semaphore()
    everyone = [*wires.near, *wires.ring, *wires.peers_x]
    for peer in everyone:
        pl.semaphore_signal(barrier, inc=1, device_id=peer, device_id_type=MESH)

    lane = lax.broadcasted_iota(jnp.int32, (HEAD, LANES), 1)
    loads[0].wait()
    columns = jnp.zeros((HEAD, LANES), F32)
    for h in range(HEADS):
        feat32 = jnp.maximum(k_ref[head_rows(h), :], 0).astype(F32)
        columns = jnp.where(lane == h, lane_sums(feat32), columns)
    z.local[...] = as_rows(columns)
    pl.semaphore_wait(barrier, len(everyone))
    z.start()

    loads[1].wait()
    for h in range(HEADS):
        rows = head_rows(h)
        s_local[rows, :] = dot(jnp.maximum(k_ref[rows, :], 0), under(v_ref[rows, :], 1.0), (1, 1))
    s_local[HEADS * HEAD :, :] = jnp.zeros((ROWS - HEADS * HEAD, LANES), F32)
    s.start()
    r_local[...] = jnp.zeros((ROWS, LANES), F32)
    s.over_y()
    z.over_z()
    z.over_x()
    s.over_z()
    loads[2].wait()
    loads[3].wait()
    z.finish()
    s.over_x()

    norms = z_full[...].T[:HEAD]
    for h in range(HEADS):
        rows = head_rows(h)
        feat32 = jnp.maximum(q_ref[rows, :], 0).astype(F32)
        inv = 1.0 / (jnp.sum(feat32 * norms[:, h : h + 1], axis=0, keepdims=True) + 1.0)
        inv_ref[h : h + 1, :] = inv
        pair = dot(jnp.concatenate(halves(feat32 * inv), 0), g_ref[rows, :], (1, 1))
        r_local[rows, :HEAD] = pair[:HEAD] + pair[HEAD:]
    r.start()
    r.over_y()
    s.over_half()
    s.gather_z()
    r.over_z()
    s.gather_y()
    r.over_x()
    r.over_half()
    s.gather_core()

    def query_heads(first, count, columns):
        for n in range(count):
            h = first + n
            rows = pl.ds(pl.multiple_of(h * HEAD, 16), HEAD)
            feat32 = jnp.maximum(q_ref[rows, :], 0).astype(F32)
            inv = inv_ref[pl.ds(h, 1), :]
            state = s_full[rows, :]
            pair = dot(jnp.concatenate(halves(state[:, :HEAD]), 0), g_ref[rows, :], (1, 0))
            back = pair[:HEAD] + pair[HEAD:]
            along = jnp.sum(feat32 * back, axis=0, keepdims=True)
            grad_den = -(along * inv) * inv
            norm = state[:, HEAD : HEAD + 1]
            dq_ref[rows, :] = jnp.where(feat32 > 0, back * inv + norm * grad_den, 0.0).astype(BF16)
            columns = jnp.where(lane == h, lane_sums(feat32 * grad_den), columns)
        return columns

    early = ROWS // N_C // HEAD - 1
    columns = query_heads(wires.c * (HEADS - early), early, jnp.zeros((HEAD, LANES), F32))
    s.finish()
    columns = query_heads((1 - wires.c) * early, HEADS - early, columns)
    y.local[...] = as_rows(columns)
    y.start()
    r.gather_z()
    y.over_z()
    r.gather_y()
    y.over_x()
    r.gather_core()
    y.finish()
    r.finish()
    for copy in wires.started:
        copy.wait_send()


def key_side(k_ref, v_ref, r_ref, y_ref, dq_ref, dk_hbm, dv_hbm, dq_hbm, dk_ref, dv_ref, io):
    norms = y_ref[...].T[:HEAD]
    copies = [pltpu.make_async_copy(dq_ref, dq_hbm, io.at[0])]
    copies[0].start()
    for h in range(HEADS):
        rows = head_rows(h)
        feat = jnp.maximum(k_ref[rows, :], 0)
        state = r_ref[rows, :]
        pair = dot(jnp.concatenate(halves(state), 1), feat, (0, 0))
        dv_ref[rows, :] = (pair[:HEAD] + pair[LANES : LANES + HEAD]).astype(BF16)
        pair = dot(jnp.concatenate(halves(state[:, :HEAD]), 0), v_ref[rows, :], (1, 0))
        grad_k = pair[:HEAD] + pair[HEAD:] + norms[:, h : h + 1]
        dk_ref[rows, :] = jnp.where(feat.astype(F32) > 0, grad_k, 0.0).astype(BF16)
        if h % GROUP == GROUP - 1:
            done = pl.ds(HEAD * (h + 1 - GROUP), HEAD * GROUP)
            for src, dst in ((dk_ref, dk_hbm), (dv_ref, dv_hbm)):
                copies.append(pltpu.make_async_copy(src.at[done], dst.at[done], io.at[len(copies)]))
                copies[-1].start()
    for copy in copies:
        copy.wait()


def on_device(queries, keys, values, out_grad):
    queries, keys, values, out_grad = queries.T, keys.T, values.T, out_grad.T
    width, tokens = queries.shape
    like = jax.ShapeDtypeStruct((width, tokens), BF16)
    anywhere = pl.BlockSpec(memory_space=pl.ANY)
    hbm = pl.BlockSpec(memory_space=pltpu.HBM)
    vmem = pl.BlockSpec(memory_space=pltpu.VMEM)
    query_grad, r_full, y_full = pl.pallas_call(
        whole,
        out_shape=(like, jax.ShapeDtypeStruct((ROWS, LANES), F32), jax.ShapeDtypeStruct((SMALL, LANES), F32)),
        in_specs=[hbm] * 4,
        out_specs=(vmem, vmem, vmem),
        scratch_shapes=[
            *[pltpu.VMEM((width, tokens), BF16)] * 4,
            *[pltpu.VMEM((ROWS, LANES), F32)] * 3,
            pltpu.VMEM((SMALL, LANES), F32),
            pltpu.VMEM((SMALL, tokens), F32),
            pltpu.SemaphoreType.DMA((4,)),
            *Flow.SCRATCH, *Flow.SCRATCH, *Small.SCRATCH, *Small.SCRATCH,
        ],
        compiler_params=pltpu.CompilerParams(
            collective_id=0, has_side_effects=True, vmem_limit_bytes=WHOLE_VMEM
        ),
        name="whole",
    )(*[pltpu.with_memory_space_constraint(a, pltpu.HBM) for a in (keys, values, queries, out_grad)])
    key_grad, value_grad, query_grad = pl.pallas_call(
        key_side,
        out_shape=(like, like, like),
        in_specs=[vmem] * 5,
        out_specs=(anywhere, anywhere, anywhere),
        scratch_shapes=[
            *[pltpu.VMEM((width, tokens), BF16)] * 2,
            pltpu.SemaphoreType.DMA((1 + 2 * HEADS // GROUP,)),
        ],
        name="key_side",
        compiler_params=pltpu.CompilerParams(vmem_limit_bytes=LAST_VMEM),
    )(keys, values, r_full, y_full, query_grad)
    return query_grad.T, key_grad.T, value_grad.T


def solution(mesh):
    spec = P(("tm", "space"), None)
    return jax.shard_map(
        on_device, mesh=mesh, in_specs=(spec,) * 4, out_specs=(spec,) * 3, check_vma=False
    )
```

```python
import functools

import jax
import jax.numpy as jnp
from jax import lax
from jax.experimental import pallas as pl
from jax.experimental.pallas import tpu as pltpu
from jax.sharding import PartitionSpec as P

HEADS = 20
HEAD = 112
LANES = 128
N_X, N_ZH, N_Z, N_Y, N_C = 4, 2, 4, 4, 2
BLOCK = 8 * -(-HEADS * HEAD // (8 * N_Z * N_Y * N_C))
ROWS = BLOCK * N_Z * N_Y * N_C
SMALL = 8 * -(-HEADS // 8)
GROUP = 4
WHOLE_VMEM = 26 * 1024 * 1024
LAST_VMEM = 24 * 1024 * 1024
MESH = pl.DeviceIdType.MESH
F32, BF16 = jnp.float32, jnp.bfloat16
ORDER = [*range(1, N_Z), 0]


def halves(x):
    high = x.astype(BF16)
    low = (x - high.astype(F32)).astype(BF16)
    return high, low


def dot(a, b, contract):
    return lax.dot_general(a, b, ((contract[:1], contract[1:]), ((), ())), preferred_element_type=F32)


def head_rows(h):
    return slice(HEAD * h, HEAD * (h + 1))


def under(rows, first):
    rest = jnp.zeros((LANES - HEAD, rows.shape[1]), F32)
    at = lax.broadcasted_iota(jnp.int32, rest.shape, 0)
    return jnp.concatenate([rows, jnp.where(at == 0, first, rest).astype(rows.dtype)], 0)


def lane_sums(x):
    parts = [x[:, at : at + LANES] for at in range(0, x.shape[1], LANES)]
    return jnp.sum(sum(parts[1:], parts[0]), axis=1, keepdims=True)


def as_rows(columns):
    blank = jnp.zeros((LANES - HEAD, LANES), F32)
    return jnp.concatenate([columns, blank], 0).T[:SMALL]


def turn(v, k, n):
    return lax.rem(v + (k + n), n)


def far_first(peers):
    n = len(peers) + 1
    return sorted(enumerate(peers), key=lambda item: -min(item[0] + 1, n - item[0] - 1))


class Wires:
    def __init__(self):
        tm, space = lax.axis_index("tm"), lax.axis_index("space")
        self.zh, self.x = lax.div(tm, N_X), lax.rem(tm, N_X)
        self.z, rest = lax.div(space, N_Y * N_C), lax.rem(space, N_Y * N_C)
        self.y, self.c = lax.div(rest, N_C), lax.rem(rest, N_C)
        self.started = []
        self.mate = self.at(c=1 - self.c)
        self.other = self.at(zh=1 - self.zh)
        self.peers_y = [self.at(y=turn(self.y, j, N_Y)) for j in range(1, N_Y)]
        self.peers_z = [self.at(z=turn(self.z, j, N_Z)) for j in range(1, N_Z)]
        self.peers_x = [self.at(x=turn(self.x, j, N_X)) for j in range(1, N_X)]
        self.near = [
            self.at(y=turn(self.y, j, N_Y), c=turn(self.c, i, N_C))
            for j in range(N_Y) for i in range(N_C) if i or j
        ]
        depth = self.zh * N_Z + self.z
        self.ring = []
        for k in range(1, N_ZH * N_Z):
            d = turn(depth, k, N_ZH * N_Z)
            self.ring.append(self.at(zh=lax.div(d, N_Z), z=lax.rem(d, N_Z)))
        self.same_half = [
            lax.div(turn(depth, -k, N_ZH * N_Z), N_Z) == self.zh for k in range(1, N_ZH * N_Z)
        ]

    def at(self, **moved):
        zh, x, z, y, c = (moved.get(n, getattr(self, n, None)) for n in ("zh", "x", "z", "y", "c"))
        return (zh * N_X + x, (z * N_Y + y) * N_C + c)

    def send(self, src, dst, send_sem, recv_sem, peer):
        copy = pltpu.make_async_remote_copy(
            src_ref=src, dst_ref=dst, send_sem=send_sem, recv_sem=recv_sem, device_id=peer, device_id_type=MESH
        )
        copy.start()
        self.started.append(copy)
        return copy


def block(ref, c, z, y=None):
    start = (c * N_Z + z) * N_Y
    if y is None:
        return ref.at[pl.ds(pl.multiple_of(start * BLOCK, 8), N_Y * BLOCK)]
    return ref.at[pl.ds(pl.multiple_of((start + y) * BLOCK, 8), BLOCK)]


class Flow:
    SCRATCH = [
        pltpu.VMEM((N_Z, N_Y * BLOCK, LANES), F32),
        pltpu.VMEM((N_Z, N_Y * BLOCK, LANES), F32),
        pltpu.VMEM((N_Z * (N_Y - 1), BLOCK, LANES), F32),
        pltpu.VMEM((N_Z, BLOCK, LANES), F32),
        pltpu.VMEM((N_Z - 1, BLOCK, LANES), F32),
        pltpu.VMEM((BLOCK, LANES), F32),
        pltpu.VMEM((N_X - 1, BLOCK, LANES), F32),
        pltpu.VMEM((BLOCK, LANES), F32),
        pltpu.VMEM((BLOCK, LANES), F32),
        pltpu.SemaphoreType.DMA((42,)),
        pltpu.SemaphoreType.DMA((42,)),
    ]

    def __init__(self, wires, reverse, local, full, scratch):
        self.w, self.reverse, self.local, self.full = wires, reverse, local, full
        (self.from_core, self.on_chip, self.from_y, self.to_z, self.from_z, self.share, self.from_x,
         self.total, self.from_half, self.sent, self.got) = scratch
        self.column = {k: turn(wires.z, k, N_Z) for k in ORDER}
        self.source = {k: turn(wires.z, -k, N_Z) for k in range(N_Z)}

    def send(self, src, dst, n, peer):
        return self.w.send(src, dst, self.sent.at[n], self.got.at[n], peer)

    def start(self):
        w = self.w
        self.core = {
            k: self.send(block(self.local, 1 - w.c, self.column[k]), self.from_core.at[k], k, w.mate) for k in ORDER
        }

    def over_y(self):
        w = self.w
        self.over = {}
        for k in ORDER:
            self.core[k].wait_recv()
            self.on_chip[k] = block(self.local, w.c, self.column[k])[...] + self.from_core[k]
            for j, peer in far_first(w.peers_y):
                slot = k * (N_Y - 1) + j
                piece = pl.ds(pl.multiple_of(turn(w.y, j + 1, N_Y) * BLOCK, 8), BLOCK)
                self.over[k, j] = self.send(self.on_chip.at[k, piece], self.from_y.at[slot], 4 + slot, peer)

    def over_z(self):
        w = self.w
        self.line = []
        mine = pl.ds(pl.multiple_of(w.y * BLOCK, 8), BLOCK)
        for k in ORDER:
            value = self.on_chip[k, mine]
            for j in range(N_Y - 1):
                self.over[k, j].wait_recv()
                value = value + self.from_y[k * (N_Y - 1) + j]
            self.to_z[k] = value
            if k:
                self.line.append(self.send(self.to_z.at[k], self.from_z.at[k - 1], 15 + k, w.peers_z[k - 1]))

    def over_x(self):
        value = self.to_z[0]
        for j, copy in enumerate(self.line):
            copy.wait_recv()
            value = value + self.from_z[j]
        self.share[...] = value
        self.rows = {j: self.send(self.share, self.from_x.at[j], 19 + j, p) for j, p in far_first(self.w.peers_x)}

    def over_half(self):
        value = self.share[...]
        for j, copy in self.rows.items():
            copy.wait_recv()
            value = value + self.from_x[j]
        self.total[...] = value
        self.cross = self.send(self.total, self.from_half, 22, self.w.other)

    def gather_z(self):
        w = self.w
        value = self.share[...]
        for j in range(N_X - 1):
            wanted = w.x < j + 1 if self.reverse else w.x >= j + 1
            value = value + jnp.where(wanted, self.from_x[j], 0.0)
        self.cross.wait_recv()
        value = value + jnp.where(w.zh == (0 if self.reverse else 1), self.from_half[...], 0.0)
        mine = block(self.full, w.c, w.z, w.y)
        mine[...] = value
        self.spread = {j + 1: self.send(mine, mine, 23 + j, p) for j, p in far_first(w.peers_z)}
        self.over = {}
        self.gather_y(range(1))

    def gather_y(self, which=range(1, N_Z)):
        w = self.w
        for k in which:
            if k:
                self.spread[k].wait_recv()
            piece = block(self.full, w.c, self.source[k], w.y)
            for j, peer in far_first(w.peers_y):
                slot = k * (N_Y - 1) + j
                self.over[k, j] = self.send(piece, piece, 26 + slot, peer)

    def gather_core(self):
        w = self.w
        self.last = []
        for k in range(N_Z):
            for j in range(N_Y - 1):
                self.over[k, j].wait_recv()
            piece = block(self.full, w.c, self.source[k])
            self.last.append(self.send(piece, piece, 38 + k, w.mate))

    def finish(self):
        for copy in self.last:
            copy.wait_recv()


class Small:
    SCRATCH = [
        pltpu.VMEM((SMALL, LANES), F32),
        pltpu.VMEM((N_Y * N_C - 1, SMALL, LANES), F32),
        pltpu.VMEM((SMALL, LANES), F32),
        pltpu.VMEM((N_ZH * N_Z - 1, SMALL, LANES), F32),
        pltpu.VMEM((2, SMALL, LANES), F32),
        pltpu.VMEM((N_X - 1, 2, SMALL, LANES), F32),
        pltpu.SemaphoreType.DMA((17,)),
        pltpu.SemaphoreType.DMA((17,)),
    ]

    def __init__(self, wires, reverse, full, scratch):
        self.w, self.reverse, self.full = wires, reverse, full
        self.local, self.from_near, self.near, self.from_ring, self.both, self.from_x, self.sent, self.got = scratch

    def send(self, src, dst, n, peer):
        return self.w.send(src, dst, self.sent.at[n], self.got.at[n], peer)

    def start(self):
        order = sorted(enumerate(self.w.near), key=lambda item: abs((item[0] + 1) // N_C - N_Y // 2))
        self.copies = {j: self.send(self.local, self.from_near.at[j], j, peer) for j, peer in order}

    def over_z(self):
        value = self.local[...]
        for j, copy in self.copies.items():
            copy.wait_recv()
            value = value + self.from_near[j]
        self.near[...] = value
        self.copies = {
            j: self.send(self.near, self.from_ring.at[j], 7 + j, peer) for j, peer in far_first(self.w.ring)
        }

    def over_x(self):
        here, there = self.near[...], jnp.zeros((SMALL, LANES), F32)
        for j, copy in self.copies.items():
            copy.wait_recv()
            piece, same = self.from_ring[j], self.w.same_half[j]
            here = here + jnp.where(same, piece, 0.0)
            there = there + jnp.where(same, 0.0, piece)
        self.both[0] = here
        self.both[1] = there
        self.copies = {
            j: self.send(self.both, self.from_x.at[j], 14 + j, peer) for j, peer in far_first(self.w.peers_x)
        }

    def finish(self):
        w = self.w
        value, far = self.both[0], self.both[1]
        for j, copy in self.copies.items():
            copy.wait_recv()
            wanted = w.x < j + 1 if self.reverse else w.x >= j + 1
            value = value + jnp.where(wanted, self.from_x[j, 0], 0.0)
            far = far + self.from_x[j, 1]
        self.full[...] = value + jnp.where(w.zh == (0 if self.reverse else 1), far, 0.0)


N_FLOW, N_SMALL = len(Flow.SCRATCH), len(Small.SCRATCH)


def whole(k_hbm, v_hbm, q_hbm, g_hbm, dq_ref, r_full, y_full, *scratch):
    k_ref, v_ref, q_ref, g_ref, s_local, r_local, s_full, z_full, inv_ref, io = scratch[:10]
    scratch = scratch[10:]
    loads = [
        pltpu.make_async_copy(src, dst, io.at[n])
        for n, (src, dst) in enumerate([(k_hbm, k_ref), (v_hbm, v_ref), (q_hbm, q_ref), (g_hbm, g_ref)])
    ]
    for load in loads:
        load.start()
    wires = Wires()
    s = Flow(wires, False, s_local, s_full, scratch[:N_FLOW])
    r = Flow(wires, True, r_local, r_full, scratch[N_FLOW : 2 * N_FLOW])
    z = Small(wires, False, z_full, scratch[2 * N_FLOW : 2 * N_FLOW + N_SMALL])
    y = Small(wires, True, y_full, scratch[2 * N_FLOW + N_SMALL :])

    barrier = pltpu.get_barrier_semaphore()
    everyone = [*wires.near, *wires.ring, *wires.peers_x]
    for peer in everyone:
        pl.semaphore_signal(barrier, inc=1, device_id=peer, device_id_type=MESH)

    lane = lax.broadcasted_iota(jnp.int32, (HEAD, LANES), 1)
    loads[0].wait()
    columns = jnp.zeros((HEAD, LANES), F32)
    for h in range(HEADS):
        feat32 = jnp.maximum(k_ref[head_rows(h), :], 0).astype(F32)
        columns = jnp.where(lane == h, lane_sums(feat32), columns)
    z.local[...] = as_rows(columns)
    pl.semaphore_wait(barrier, len(everyone))
    z.start()

    loads[1].wait()
    for h in range(HEADS):
        rows = head_rows(h)
        s_local[rows, :] = dot(jnp.maximum(k_ref[rows, :], 0), under(v_ref[rows, :], 1.0), (1, 1))
    s_local[HEADS * HEAD :, :] = jnp.zeros((ROWS - HEADS * HEAD, LANES), F32)
    s.start()
    r_local[...] = jnp.zeros((ROWS, LANES), F32)
    s.over_y()
    z.over_z()
    z.over_x()
    s.over_z()
    loads[2].wait()
    loads[3].wait()
    z.finish()
    s.over_x()

    norms = z_full[...].T[:HEAD]
    for h in range(HEADS):
        rows = head_rows(h)
        feat32 = jnp.maximum(q_ref[rows, :], 0).astype(F32)
        inv = 1.0 / (jnp.sum(feat32 * norms[:, h : h + 1], axis=0, keepdims=True) + 1.0)
        inv_ref[h : h + 1, :] = inv
        pair = dot(jnp.concatenate(halves(feat32 * inv), 0), g_ref[rows, :], (1, 1))
        r_local[rows, :HEAD] = pair[:HEAD] + pair[HEAD:]
    r.start()
    r.over_y()
    s.over_half()
    s.gather_z()
    r.over_z()
    s.gather_y()
    r.over_x()
    r.over_half()
    s.gather_core()

    def query_heads(first, count, columns):
        for n in range(count):
            h = first + n
            rows = pl.ds(pl.multiple_of(h * HEAD, 16), HEAD)
            feat32 = jnp.maximum(q_ref[rows, :], 0).astype(F32)
            inv = inv_ref[pl.ds(h, 1), :]
            state = s_full[rows, :]
            pair = dot(jnp.concatenate(halves(state[:, :HEAD]), 0), g_ref[rows, :], (1, 0))
            back = pair[:HEAD] + pair[HEAD:]
            along = jnp.sum(feat32 * back, axis=0, keepdims=True)
            grad_den = -(along * inv) * inv
            norm = state[:, HEAD : HEAD + 1]
            dq_ref[rows, :] = jnp.where(feat32 > 0, back * inv + norm * grad_den, 0.0).astype(BF16)
            columns = jnp.where(lane == h, lane_sums(feat32 * grad_den), columns)
        return columns

    early = ROWS // N_C // HEAD - 1
    columns = query_heads(wires.c * (HEADS - early), early, jnp.zeros((HEAD, LANES), F32))
    s.finish()
    columns = query_heads((1 - wires.c) * early, HEADS - early, columns)
    y.local[...] = as_rows(columns)
    y.start()
    r.gather_z()
    y.over_z()
    r.gather_y()
    y.over_x()
    r.gather_core()
    y.finish()
    r.finish()
    for copy in wires.started:
        copy.wait_send()


def key_side(k_ref, v_ref, r_ref, y_ref, dq_ref, dk_hbm, dv_hbm, dq_hbm, dk_ref, dv_ref, io):
    norms = y_ref[...].T[:HEAD]
    copies = [pltpu.make_async_copy(dq_ref, dq_hbm, io.at[0])]
    copies[0].start()
    for h in range(HEADS):
        rows = head_rows(h)
        feat = jnp.maximum(k_ref[rows, :], 0)
        state = r_ref[rows, :]
        pair = dot(jnp.concatenate(halves(state), 1), feat, (0, 0))
        dv_ref[rows, :] = (pair[:HEAD] + pair[LANES : LANES + HEAD]).astype(BF16)
        pair = dot(jnp.concatenate(halves(state[:, :HEAD]), 0), v_ref[rows, :], (1, 0))
        grad_k = pair[:HEAD] + pair[HEAD:] + norms[:, h : h + 1]
        dk_ref[rows, :] = jnp.where(feat.astype(F32) > 0, grad_k, 0.0).astype(BF16)
        if h % GROUP == GROUP - 1:
            done = pl.ds(HEAD * (h + 1 - GROUP), HEAD * GROUP)
            for src, dst in ((dk_ref, dk_hbm), (dv_ref, dv_hbm)):
                copies.append(pltpu.make_async_copy(src.at[done], dst.at[done], io.at[len(copies)]))
                copies[-1].start()
    for copy in copies:
        copy.wait()


def on_device(queries, keys, values, out_grad):
    queries, keys, values, out_grad = queries.T, keys.T, values.T, out_grad.T
    width, tokens = queries.shape
    like = jax.ShapeDtypeStruct((width, tokens), BF16)
    anywhere = pl.BlockSpec(memory_space=pl.ANY)
    hbm = pl.BlockSpec(memory_space=pltpu.HBM)
    vmem = pl.BlockSpec(memory_space=pltpu.VMEM)
    query_grad, r_full, y_full = pl.pallas_call(
        whole,
        out_shape=(like, jax.ShapeDtypeStruct((ROWS, LANES), F32), jax.ShapeDtypeStruct((SMALL, LANES), F32)),
        in_specs=[hbm] * 4,
        out_specs=(vmem, vmem, vmem),
        scratch_shapes=[
            *[pltpu.VMEM((width, tokens), BF16)] * 4,
            *[pltpu.VMEM((ROWS, LANES), F32)] * 3,
            pltpu.VMEM((SMALL, LANES), F32),
            pltpu.VMEM((SMALL, tokens), F32),
            pltpu.SemaphoreType.DMA((4,)),
            *Flow.SCRATCH, *Flow.SCRATCH, *Small.SCRATCH, *Small.SCRATCH,
        ],
        compiler_params=pltpu.CompilerParams(
            collective_id=0, has_side_effects=True, vmem_limit_bytes=WHOLE_VMEM
        ),
        name="whole",
    )(*[pltpu.with_memory_space_constraint(a, pltpu.HBM) for a in (keys, values, queries, out_grad)])
    key_grad, value_grad, query_grad = pl.pallas_call(
        key_side,
        out_shape=(like, like, like),
        in_specs=[vmem] * 5,
        out_specs=(anywhere, anywhere, anywhere),
        scratch_shapes=[
            *[pltpu.VMEM((width, tokens), BF16)] * 2,
            pltpu.SemaphoreType.DMA((1 + 2 * HEADS // GROUP,)),
        ],
        name="key_side",
        compiler_params=pltpu.CompilerParams(vmem_limit_bytes=LAST_VMEM),
    )(keys, values, r_full, y_full, query_grad)
    return query_grad.T, key_grad.T, value_grad.T


def solution(mesh):
    spec = P(("tm", "space"), None)
    return jax.shard_map(
        on_device, mesh=mesh, in_specs=(spec,) * 4, out_specs=(spec,) * 3, check_vma=False
    )
```
